256 devices in a mesh: wide: 64 (over z, x, core), narrow: 4 (over y).
Axes of the slice: x: 4, y: 4, z: 8, core: 2. Of those that a mesh axis runs over, the one named last changes fastest.
Arguments:
- snapshot: float32 [512, 16, 512, 128], P('wide', 'narrow'), may hold values from -81 to 81
Outputs:
- core: float32 [256, 16, 512, 128], P(None, 'narrow', 'wide')
- factor: float32 [512, 256], replicated
The draws below stay inside these ranges and needn't reach their ends.
All inputs are finite; a program needn't handle non-finite values.
Results may differ from the reference program's by a relative error of at most 0.000071.
Values sent between devices are 32-bit elements; how exact they have to be, the bound alone decides.
A program may use at most 320 MiB of HBM per device.

```python
import math
import jax
import jax.numpy as jnp
from jax import lax

NX = 512
RANK = 256
FIELDS = 128
NY = 16
NZ = 512


def draw_snapshot(key, part):
    keys = jax.random.split(jax.random.fold_in(key, 11), 4)
    noise = jnp.clip(jax.random.normal(keys[0], (NX, NY, NZ, FIELDS), jnp.float32), -6.0, 6.0)
    shared = jnp.clip(jax.random.normal(keys[3], (1, NY, NZ, FIELDS), jnp.float32), -6.0, 6.0)
    row_scale = 0.3 * jnp.exp(jax.random.uniform(keys[1], (NX, 1, 1, 1), jnp.float32, 0.0, math.log(10.0)))
    mixing = jnp.clip(0.1 * jax.random.normal(keys[2], (NX, 1, 1, 1), jnp.float32), -0.5, 0.5)
    depth = jnp.arange(NZ, dtype=jnp.float32).reshape(1, 1, NZ, 1)
    z_scale = 1.0 + 2.0 * depth / max(NZ - 1, 1)
    return row_scale * z_scale * (noise + mixing * shared)


def setup_inputs(seed: int = 0) -> dict:
    arg_keys = jax.random.split(jax.random.key(seed), 2)
    snapshot = draw_snapshot(jax.random.fold_in(arg_keys[1], 71), 0)
    return {"snapshot": snapshot}


def reference(snapshot):
    unfold = snapshot.reshape(NX, -1)
    gram = jnp.dot(unfold.astype(jnp.float32), unfold.T.astype(jnp.float32), precision=lax.Precision.HIGHEST, preferred_element_type=jnp.float32)
    upper = jnp.linalg.cholesky(gram).T
    rows_kept = upper[:RANK, :]
    lengths = jnp.sqrt(lax.optimization_barrier(jnp.sum(rows_kept * rows_kept, axis=1)))
    factor = (rows_kept / lengths[:, None]).T
    core = jnp.dot(factor.T.astype(jnp.float32), unfold.astype(jnp.float32), precision=lax.Precision.HIGHEST, preferred_element_type=jnp.float32)
    return (core.reshape(RANK, NY, NZ, FIELDS), factor)
```

```python
import functools

import jax
import jax.numpy as jnp
from jax import lax
from jax.experimental import pallas as pl
from jax.experimental.pallas import tpu as pltpu
from jax.sharding import PartitionSpec as P

RANK = 256
ROWS = 512
NZD, NXD, NCD, NYD = 8, 4, 2, 4
WIDE = NZD * NXD * NCD
CHUNKS = 8
MESH = pl.DeviceIdType.MESH
HIGHEST = lax.Precision.HIGHEST


def exchange_gram_kernel(
    x_ref, u_ref, g_ref,
    xin, stag, ubuf, gacc, r1, h2, r2, r3, gfull,
    in_sem, a_send, a_recv, out_sem, red_send, red_recv,
):
    w = lax.axis_index("wide")
    y = lax.axis_index("narrow")
    z, x, c = w // 8, (w // 2) % 4, w % 2
    piece = x * NYD + y

    def wide_id(zz, xx, cc):
        return zz * 8 + xx * 2 + cc

    barrier = pltpu.get_barrier_semaphore()

    def greet(i, carry):
        pl.semaphore_signal(barrier, inc=1, device_id=((w + i) % WIDE, y), device_id_type=MESH)
        return carry

    lax.fori_loop(1, WIDE, greet, 0)

    def greet_plane(i, carry):
        yy, xx = (y + 1 + i // NXD) % NYD, i % NXD
        pl.semaphore_signal(
            barrier, inc=1, device_id=(wide_id(z, xx, c), yy), device_id_type=MESH
        )
        return carry

    lax.fori_loop(0, (NYD - 1) * NXD, greet_plane, 0)

    def load(i, carry):
        yy, r = i // 8, i % 8
        pltpu.make_async_copy(
            x_ref.at[r, yy], xin.at[pl.ds(pl.multiple_of(i * 512, 512), 512)], in_sem.at[yy]
        ).start()
        return carry

    lax.fori_loop(0, 32, load, 0)

    def relayout(ch):
        yy, zh = ch // 2, ch % 2
        base = yy * 4096 + zh * 4

        def body(d, carry):
            for q in range(4):
                stag[ch, d, q] = xin[pl.ds(base + d * 8 + q, 8, stride=512), :]
            return carry

        lax.fori_loop(0, WIDE, body, 0, unroll=4)
        for q in range(4):
            ubuf[ch, q, w] = stag[ch, w, q]

    def wait_in(yy):
        whole = xin.at[pl.ds(pl.multiple_of(yy * 4096, 4096), 4096)]
        pltpu.make_async_copy(whole, whole, in_sem.at[yy]).wait()

    def send(ch):
        def body(i, carry):
            off = (i * 27) % WIDE
            t = wide_id((z + off // 8) % NZD, (x + (off // 2) % 4) % NXD, (c + off % 2) % NCD)
            pltpu.make_async_remote_copy(
                src_ref=stag.at[ch, t],
                dst_ref=ubuf.at[ch, :, w],
                send_sem=a_send.at[ch],
                recv_sem=a_recv.at[ch],
                device_id=(t, y),
                device_id_type=MESH,
            ).start()
            return carry

        lax.fori_loop(1, WIDE, body, 0)

    wait_in(0)
    relayout(0)
    pl.semaphore_wait(barrier, WIDE - 1 + (NYD - 1) * NXD)
    send(0)
    relayout(1)
    send(1)

    def send_two(yy, carry):
        wait_in(yy)
        for zh in range(2):
            relayout(yy * 2 + zh)
            send(yy * 2 + zh)
        return carry

    lax.fori_loop(1, 4, send_two, 0)

    gacc[...] = jnp.zeros_like(gacc)

    def gram(ch, carry):
        got = ubuf.at[ch, :, pl.ds(0, WIDE - 1)]
        pltpu.make_async_copy(got, got, a_recv.at[ch]).wait()
        pltpu.make_async_copy(ubuf.at[ch], u_ref.at[ch], out_sem.at[ch]).start()
        for q in range(0, 4, 2):
            left = ubuf[ch, q].reshape(ROWS, 128)
            right = ubuf[ch, q + 1].reshape(ROWS, 128)
            a = jnp.concatenate([left, right], axis=1)
            part = lax.dot_general(
                a, a[:RANK], (((1,), (1,)), ((), ())),
                precision=HIGHEST, preferred_element_type=jnp.float32,
            )
            gacc[...] += part.reshape(2, 16, 16, RANK)
        return carry

    lax.fori_loop(0, CHUNKS, gram, 0)

    partner = wide_id(z, x, 1 - c)
    pltpu.make_async_remote_copy(
        src_ref=gacc.at[1 - c], dst_ref=r1, send_sem=red_send.at[0], recv_sem=red_recv.at[0],
        device_id=(partner, y), device_id_type=MESH,
    ).start()
    pltpu.make_async_copy(r1, r1, red_recv.at[0]).wait()
    h2[...] = gacc[c] + r1[...]

    def plane(i, stage, source, target):
        t = (piece + i) % 16
        pltpu.make_async_remote_copy(
            src_ref=source(t), dst_ref=target, send_sem=red_send.at[stage],
            recv_sem=red_recv.at[stage], device_id=(wide_id(z, t // NYD, c), t % NYD),
            device_id_type=MESH,
        ).start()

    def scatter(i, carry):
        plane(i, 1, lambda t: h2.at[t], r2.at[piece])
        return carry

    lax.fori_loop(1, 16, scatter, 0)
    r2[piece] = h2[piece]
    got = r2.at[pl.ds(0, 15)]
    pltpu.make_async_copy(got, got, red_recv.at[1]).wait()
    total = r2[0]
    for i in range(1, 16):
        total = total + r2[i]
    r3[z] = total

    def along_z(i, carry):
        zz = (z + i) % NZD
        pltpu.make_async_remote_copy(
            src_ref=r3.at[z], dst_ref=r3.at[z], send_sem=red_send.at[2],
            recv_sem=red_recv.at[2], device_id=(wide_id(zz, x, c), y), device_id_type=MESH,
        ).start()
        return carry

    lax.fori_loop(1, NZD, along_z, 0)
    got = r3.at[pl.ds(0, NZD - 1)]
    pltpu.make_async_copy(got, got, red_recv.at[2]).wait()
    total = r3[0]
    for i in range(1, NZD):
        total = total + r3[i]
    gfull[c, piece] = total

    def gather(i, carry):
        plane(i, 3, lambda t: gfull.at[c, piece], gfull.at[c, piece])
        return carry

    lax.fori_loop(1, 16, gather, 0)
    got = gfull.at[c, pl.ds(0, 15)]
    pltpu.make_async_copy(got, got, red_recv.at[3]).wait()
    pltpu.make_async_remote_copy(
        src_ref=gfull.at[c], dst_ref=gfull.at[c], send_sem=red_send.at[4],
        recv_sem=red_recv.at[4], device_id=(partner, y), device_id_type=MESH,
    ).start()
    pltpu.make_async_copy(gfull.at[0], gfull.at[0], red_recv.at[4]).wait()
    g_ref[...] = gfull[...].reshape(ROWS, RANK)

    def drain(ch, carry):
        sent = stag.at[ch, pl.ds(0, WIDE - 1)]
        pltpu.make_async_copy(sent, sent, a_send.at[ch]).wait()
        pltpu.make_async_copy(ubuf.at[ch], u_ref.at[ch], out_sem.at[ch]).wait()
        return carry

    lax.fori_loop(0, CHUNKS, drain, 0)
    pltpu.make_async_copy(r1, r1, red_send.at[0]).wait()
    sent = h2.at[pl.ds(0, 15)]
    pltpu.make_async_copy(sent, sent, red_send.at[1]).wait()
    sent = r3.at[pl.ds(0, NZD - 1)]
    pltpu.make_async_copy(sent, sent, red_send.at[2]).wait()
    sent = gfull.at[c, pl.ds(0, 15)]
    pltpu.make_async_copy(sent, sent, red_send.at[3]).wait()
    pltpu.make_async_copy(gfull.at[0], gfull.at[0], red_send.at[4]).wait()


def exchange_gram(snapshot):
    f32 = jnp.float32
    dma = pltpu.SemaphoreType.DMA
    return pl.pallas_call(
        exchange_gram_kernel,
        name="exchange_gram",
        out_shape=(
            jax.ShapeDtypeStruct((CHUNKS, 4, WIDE, 8, 128), f32),
            jax.ShapeDtypeStruct((ROWS, RANK), f32),
        ),
        in_specs=[pl.BlockSpec(memory_space=pl.ANY)],
        out_specs=(
            pl.BlockSpec(memory_space=pl.ANY),
            pl.BlockSpec(memory_space=pltpu.VMEM),
        ),
        scratch_shapes=[
            pltpu.VMEM((4 * 8 * 512, 128), f32),
            pltpu.VMEM((CHUNKS, WIDE, 4, 8, 128), f32),
            pltpu.VMEM((CHUNKS, 4, WIDE, 8, 128), f32),
            pltpu.VMEM((2, 16, 16, RANK), f32),
            pltpu.VMEM((16, 16, RANK), f32),
            pltpu.VMEM((16, 16, RANK), f32),
            pltpu.VMEM((16, 16, RANK), f32),
            pltpu.VMEM((NZD, 16, RANK), f32),
            pltpu.VMEM((2, 16, 16, RANK), f32),
            dma((4,)), dma((CHUNKS,)), dma((CHUNKS,)), dma((CHUNKS,)), dma((5,)), dma((5,)),
        ],
        compiler_params=pltpu.CompilerParams(
            collective_id=0, has_side_effects=True, vmem_limit_bytes=48 << 20
        ),
    )(snapshot)


def core_kernel(u_ref, f_ref, core_ref):
    ft = f_ref[...]
    fh = ft.astype(jnp.bfloat16)
    fl = (ft - fh.astype(jnp.float32)).astype(jnp.bfloat16)
    dims = (((1,), (0,)), ((), ()))
    dot = functools.partial(lax.dot_general, dimension_numbers=dims, preferred_element_type=jnp.float32)
    for zz in range(0, 8, 2):
        a = jnp.concatenate(
            [u_ref[(zz + k) // 4, (zz + k) % 4].reshape(ROWS, 128) for k in range(2)], axis=1
        )
        ah = a.astype(jnp.bfloat16)
        al = (a - ah.astype(jnp.float32)).astype(jnp.bfloat16)
        out = dot(fh, ah) + (dot(fh, al) + dot(fl, ah))
        core_ref[:, 0, zz, :] = out[:, :128]
        core_ref[:, 0, zz + 1, :] = out[:, 128:]


def project(u, ft):
    f32 = jnp.float32
    return pl.pallas_call(
        core_kernel,
        name="project",
        grid=(4,),
        out_shape=jax.ShapeDtypeStruct((RANK, 4, 8, 128), f32),
        in_specs=[
            pl.BlockSpec((2, 4, WIDE, 8, 128), lambda i: (i, 0, 0, 0, 0)),
            pl.BlockSpec((RANK, ROWS), lambda i: (0, 0)),
        ],
        out_specs=pl.BlockSpec((RANK, 1, 8, 128), lambda i: (0, i, 0, 0)),
        compiler_params=pltpu.CompilerParams(vmem_limit_bytes=48 << 20),
    )(u, ft)


def on_device(snapshot):
    u, gram = exchange_gram(snapshot)
    low = jnp.linalg.cholesky(gram[:RANK])
    rows = lax.linalg.triangular_solve(low, gram.T, left_side=True, lower=True)
    rows = jnp.concatenate([low.T, rows[:, RANK:]], axis=1)
    lengths = jnp.sqrt(jnp.sum(rows * rows, axis=1))
    ft = rows / lengths[:, None]
    core = project(u, ft)
    return (core, ft.T)


def solution(mesh):
    in_specs = (P("wide", "narrow", None, None),)
    out_specs = (P(None, "narrow", "wide", None), P())
    return jax.shard_map(
        on_device, mesh=mesh, in_specs=in_specs, out_specs=out_specs, check_vma=False
    )
```

```python
import functools

import jax
import jax.numpy as jnp
from jax import lax
from jax.experimental import pallas as pl
from jax.experimental.pallas import tpu as pltpu
from jax.sharding import PartitionSpec as P

RANK = 256
ROWS = 512
NZD, NXD, NCD, NYD = 8, 4, 2, 4
WIDE = NZD * NXD * NCD
CHUNKS = 8
MESH = pl.DeviceIdType.MESH
HIGHEST = lax.Precision.HIGHEST


def exchange_gram_kernel(
    x_ref, u_ref, g_ref,
    xin, stag, ubuf, gacc, r1, h2, r2, r3, gfull,
    in_sem, a_send, a_recv, out_sem, red_send, red_recv,
):
    w = lax.axis_index("wide")
    y = lax.axis_index("narrow")
    z, x, c = w // 8, (w // 2) % 4, w % 2
    piece = x * NYD + y

    def wide_id(zz, xx, cc):
        return zz * 8 + xx * 2 + cc

    barrier = pltpu.get_barrier_semaphore()

    def greet(i, carry):
        pl.semaphore_signal(barrier, inc=1, device_id=((w + i) % WIDE, y), device_id_type=MESH)
        return carry

    lax.fori_loop(1, WIDE, greet, 0)

    def greet_plane(i, carry):
        yy, xx = (y + 1 + i // NXD) % NYD, i % NXD
        pl.semaphore_signal(
            barrier, inc=1, device_id=(wide_id(z, xx, c), yy), device_id_type=MESH
        )
        return carry

    lax.fori_loop(0, (NYD - 1) * NXD, greet_plane, 0)

    def load(i, carry):
        yy, r = i // 8, i % 8
        pltpu.make_async_copy(
            x_ref.at[r, yy], xin.at[pl.ds(pl.multiple_of(i * 512, 512), 512)], in_sem.at[yy]
        ).start()
        return carry

    lax.fori_loop(0, 32, load, 0)

    def relayout(ch):
        yy, zh = ch // 2, ch % 2
        base = yy * 4096 + zh * 4

        def body(d, carry):
            for q in range(4):
                stag[ch, d, q] = xin[pl.ds(base + d * 8 + q, 8, stride=512), :]
            return carry

        lax.fori_loop(0, WIDE, body, 0, unroll=4)
        for q in range(4):
            ubuf[ch, q, w] = stag[ch, w, q]

    def wait_in(yy):
        whole = xin.at[pl.ds(pl.multiple_of(yy * 4096, 4096), 4096)]
        pltpu.make_async_copy(whole, whole, in_sem.at[yy]).wait()

    def send(ch):
        def body(i, carry):
            off = (i * 27) % WIDE
            t = wide_id((z + off // 8) % NZD, (x + (off // 2) % 4) % NXD, (c + off % 2) % NCD)
            pltpu.make_async_remote_copy(
                src_ref=stag.at[ch, t],
                dst_ref=ubuf.at[ch, :, w],
                send_sem=a_send.at[ch],
                recv_sem=a_recv.at[ch],
                device_id=(t, y),
                device_id_type=MESH,
            ).start()
            return carry

        lax.fori_loop(1, WIDE, body, 0)

    wait_in(0)
    relayout(0)
    pl.semaphore_wait(barrier, WIDE - 1 + (NYD - 1) * NXD)
    send(0)
    relayout(1)
    send(1)

    def send_two(yy, carry):
        wait_in(yy)
        for zh in range(2):
            relayout(yy * 2 + zh)
            send(yy * 2 + zh)
        return carry

    lax.fori_loop(1, 4, send_two, 0)

    gacc[...] = jnp.zeros_like(gacc)

    def gram(ch, carry):
        got = ubuf.at[ch, :, pl.ds(0, WIDE - 1)]
        pltpu.make_async_copy(got, got, a_recv.at[ch]).wait()
        pltpu.make_async_copy(ubuf.at[ch], u_ref.at[ch], out_sem.at[ch]).start()
        for q in range(0, 4, 2):
            left = ubuf[ch, q].reshape(ROWS, 128)
            right = ubuf[ch, q + 1].reshape(ROWS, 128)
            a = jnp.concatenate([left, right], axis=1)
            part = lax.dot_general(
                a[:RANK], a, (((1,), (1,)), ((), ())),
                precision=HIGHEST, preferred_element_type=jnp.float32,
            )
            gacc[...] += part.reshape(2, 16, 8, ROWS)
        return carry

    lax.fori_loop(0, CHUNKS, gram, 0)

    partner = wide_id(z, x, 1 - c)
    pltpu.make_async_remote_copy(
        src_ref=gacc.at[1 - c], dst_ref=r1, send_sem=red_send.at[0], recv_sem=red_recv.at[0],
        device_id=(partner, y), device_id_type=MESH,
    ).start()
    pltpu.make_async_copy(r1, r1, red_recv.at[0]).wait()
    h2[...] = gacc[c] + r1[...]

    def plane(i, stage, source, target):
        t = (piece + i) % 16
        pltpu.make_async_remote_copy(
            src_ref=source(t), dst_ref=target, send_sem=red_send.at[stage],
            recv_sem=red_recv.at[stage], device_id=(wide_id(z, t // NYD, c), t % NYD),
            device_id_type=MESH,
        ).start()

    def scatter(i, carry):
        plane(i, 1, lambda t: h2.at[t], r2.at[piece])
        return carry

    lax.fori_loop(1, 16, scatter, 0)
    r2[piece] = h2[piece]
    got = r2.at[pl.ds(0, 15)]
    pltpu.make_async_copy(got, got, red_recv.at[1]).wait()
    total = r2[0]
    for i in range(1, 16):
        total = total + r2[i]
    r3[z] = total

    def along_z(i, carry):
        zz = (z + i) % NZD
        pltpu.make_async_remote_copy(
            src_ref=r3.at[z], dst_ref=r3.at[z], send_sem=red_send.at[2],
            recv_sem=red_recv.at[2], device_id=(wide_id(zz, x, c), y), device_id_type=MESH,
        ).start()
        return carry

    lax.fori_loop(1, NZD, along_z, 0)
    got = r3.at[pl.ds(0, NZD - 1)]
    pltpu.make_async_copy(got, got, red_recv.at[2]).wait()
    total = r3[0]
    for i in range(1, NZD):
        total = total + r3[i]
    gfull[c, piece] = total

    def gather(i, carry):
        plane(i, 3, lambda t: gfull.at[c, piece], gfull.at[c, piece])
        return carry

    lax.fori_loop(1, 16, gather, 0)
    got = gfull.at[c, pl.ds(0, 15)]
    pltpu.make_async_copy(got, got, red_recv.at[3]).wait()
    pltpu.make_async_remote_copy(
        src_ref=gfull.at[c], dst_ref=gfull.at[c], send_sem=red_send.at[4],
        recv_sem=red_recv.at[4], device_id=(partner, y), device_id_type=MESH,
    ).start()
    pltpu.make_async_copy(gfull.at[0], gfull.at[0], red_recv.at[4]).wait()
    g_ref[...] = gfull[...].reshape(RANK, ROWS)

    def drain(ch, carry):
        sent = stag.at[ch, pl.ds(0, WIDE - 1)]
        pltpu.make_async_copy(sent, sent, a_send.at[ch]).wait()
        pltpu.make_async_copy(ubuf.at[ch], u_ref.at[ch], out_sem.at[ch]).wait()
        return carry

    lax.fori_loop(0, CHUNKS, drain, 0)
    pltpu.make_async_copy(r1, r1, red_send.at[0]).wait()
    sent = h2.at[pl.ds(0, 15)]
    pltpu.make_async_copy(sent, sent, red_send.at[1]).wait()
    sent = r3.at[pl.ds(0, NZD - 1)]
    pltpu.make_async_copy(sent, sent, red_send.at[2]).wait()
    sent = gfull.at[c, pl.ds(0, 15)]
    pltpu.make_async_copy(sent, sent, red_send.at[3]).wait()
    pltpu.make_async_copy(gfull.at[0], gfull.at[0], red_send.at[4]).wait()


def exchange_gram(snapshot):
    f32 = jnp.float32
    dma = pltpu.SemaphoreType.DMA
    return pl.pallas_call(
        exchange_gram_kernel,
        name="exchange_gram",
        out_shape=(
            jax.ShapeDtypeStruct((CHUNKS, 4, WIDE, 8, 128), f32),
            jax.ShapeDtypeStruct((RANK, ROWS), f32),
        ),
        in_specs=[pl.BlockSpec(memory_space=pl.ANY)],
        out_specs=(
            pl.BlockSpec(memory_space=pl.ANY),
            pl.BlockSpec(memory_space=pltpu.VMEM),
        ),
        scratch_shapes=[
            pltpu.VMEM((4 * 8 * 512, 128), f32),
            pltpu.VMEM((CHUNKS, WIDE, 4, 8, 128), f32),
            pltpu.VMEM((CHUNKS, 4, WIDE, 8, 128), f32),
            pltpu.VMEM((2, 16, 8, ROWS), f32),
            pltpu.VMEM((16, 8, ROWS), f32),
            pltpu.VMEM((16, 8, ROWS), f32),
            pltpu.VMEM((16, 8, ROWS), f32),
            pltpu.VMEM((NZD, 8, ROWS), f32),
            pltpu.VMEM((2, 16, 8, ROWS), f32),
            dma((4,)), dma((CHUNKS,)), dma((CHUNKS,)), dma((CHUNKS,)), dma((5,)), dma((5,)),
        ],
        compiler_params=pltpu.CompilerParams(
            collective_id=0, has_side_effects=True, vmem_limit_bytes=48 << 20
        ),
    )(snapshot)


def unit_lower_inverse(rows):
    tile = (8, 128)
    lane = lax.broadcasted_iota(jnp.int32, tile, 1)
    sub = lax.broadcasted_iota(jnp.int32, tile, 0)
    rows, done = list(rows), []

    def lanes(v, k):
        return jnp.broadcast_to(v[:, k : k + 1], tile)

    def subs(v, k):
        return jnp.broadcast_to(v[k : k + 1, :], tile)

    for g in range(16):
        v = rows[g]
        inside = (lane >= 8 * g) & (lane < 8 * g + 8)
        cols = [lanes(v, 8 * g + k) for k in range(8)]
        a = [[subs(cols[k], i) if i >= k else None for k in range(8)] for i in range(8)]
        n = [[None] * 8 for _ in range(8)]
        m = [[None] * 8 for _ in range(8)]
        inv = [None] * 8
        for k in range(8):
            inv[k] = 1.0 / a[k][k]
            for i in range(k + 1, 8):
                m[i][k] = a[i][k] * inv[k]
                for j in range(k + 1, i + 1):
                    a[i][j] = a[i][j] - m[i][k] * a[j][k]
        for j in range(8):
            for i in range(j + 1, 8):
                s = m[i][j]
                for t in range(j + 1, i):
                    s = s + m[i][t] * n[t][j]
                n[i][j] = -s
        vt = jnp.where(inside, jnp.where(lane == 8 * g + sub, 1.0, 0.0), v)
        p = vt
        for k in range(7):
            col = jnp.zeros(tile, jnp.float32)
            for i in range(k + 1, 8):
                col = jnp.where(sub == i, n[i][k], col)
            p = p + col * subs(vt, k)
        scale = inv[0]
        for i in range(1, 8):
            scale = jnp.where(sub == i, inv[i], scale)
        q = p * scale
        qb = [subs(q, i) for i in range(8)]
        tb = []
        for j in range(8):
            s = qb[j]
            for i in range(j + 1, 8):
                s = s + n[i][j] * qb[i]
            tb.append(s)
        done.append(jnp.where(lane < 8 * g + 8, p, 0.0))
        for i in range(g + 1, 16):
            vi = rows[i]
            c = [lanes(vi, 8 * g + k) for k in range(8)]
            vi = jnp.where(inside, 0.0, vi)
            s0 = c[0] * tb[0]
            s1 = c[1] * tb[1]
            for k in range(2, 8, 2):
                s0 = s0 + c[k] * tb[k]
                s1 = s1 + c[k + 1] * tb[k + 1]
            rows[i] = vi - (s0 + s1)
    return done


def eliminate(a):
    n = a.shape[1]
    inv = jnp.concatenate(unit_lower_inverse([a[8 * g : 8 * g + 8, :128] for g in range(16)]), axis=0)
    s = jnp.dot(inv, a, precision=HIGHEST, preferred_element_type=jnp.float32)
    row = lax.broadcasted_iota(jnp.int32, (128, n), 0)
    lane = lax.broadcasted_iota(jnp.int32, (128, n), 1)
    s = jnp.where(lane >= row, s, 0.0)
    d = jnp.sum(jnp.where(lane[:, :128] == row[:, :128], s[:, :128], 0.0), axis=1, keepdims=True)
    return s, d


def unit_rows(s, d):
    r = s * (1.0 / jnp.sqrt(d))
    return r * (1.0 / jnp.sqrt(jnp.sum(r * r, axis=1, keepdims=True)))


def factor_rows(g_ref, ft_ref):
    s1, d1 = eliminate(g_ref[:128, :])
    ft_ref[:128, :] = unit_rows(s1, d1)
    right = s1[:, 128:]
    schur = lax.dot_general(right[:, :128] * (1.0 / d1), right, (((0,), (0,)), ((), ())),
        precision=HIGHEST, preferred_element_type=jnp.float32)
    s2, d2 = eliminate(g_ref[128:, 128:] - schur)
    ft_ref[128:, :128] = jnp.zeros((128, 128), jnp.float32)
    ft_ref[128:, 128:] = unit_rows(s2, d2)


def split(v):
    high = v.astype(jnp.bfloat16)
    return high, (v - high.astype(jnp.float32)).astype(jnp.bfloat16)


def core_kernel(u_ref, g_ref, core_ref, factor_ref, ft, fh, fl):
    i = pl.program_id(0)

    @pl.when(i == 0)
    def _():
        factor_rows(g_ref, ft)
        fh[...], fl[...] = split(ft[...])

    factor_ref[...] = ft[:, pl.ds(pl.multiple_of(i * 128, 128), 128)].T
    high, low = fh[...], fl[...]
    dot = functools.partial(jnp.dot, preferred_element_type=jnp.float32)
    flat = core_ref.reshape(RANK * 8, 128)
    for zz in range(0, 8, 2):
        cells = [u_ref[(zz + k) // 4, (zz + k) % 4].reshape(ROWS, 128) for k in range(2)]
        ah, al = split(jnp.concatenate(cells, axis=1))
        out = dot(high, ah) + (dot(high, al) + dot(low, ah))
        for k in range(2):
            flat[pl.ds(zz + k, RANK, stride=8), :] = out[:, 128 * k : 128 * k + 128]


def project(u, gram):
    f32 = jnp.float32
    return pl.pallas_call(
        core_kernel,
        name="project",
        grid=(NYD,),
        out_shape=(
            jax.ShapeDtypeStruct((RANK, NYD, 8, 128), f32),
            jax.ShapeDtypeStruct((ROWS, RANK), f32),
        ),
        in_specs=[
            pl.BlockSpec((2, 4, WIDE, 8, 128), lambda i: (i, 0, 0, 0, 0)),
            pl.BlockSpec((RANK, ROWS), lambda i: (0, 0)),
        ],
        out_specs=(
            pl.BlockSpec((RANK, 1, 8, 128), lambda i: (0, i, 0, 0)),
            pl.BlockSpec((128, RANK), lambda i: (i, 0)),
        ),
        scratch_shapes=[
            pltpu.VMEM((RANK, ROWS), f32),
            pltpu.VMEM((RANK, ROWS), jnp.bfloat16),
            pltpu.VMEM((RANK, ROWS), jnp.bfloat16),
        ],
        compiler_params=pltpu.CompilerParams(vmem_limit_bytes=48 << 20),
    )(u, gram)


def on_device(snapshot):
    u, gram = exchange_gram(snapshot)
    return project(u, gram)


def solution(mesh):
    in_specs = (P("wide", "narrow", None, None),)
    out_specs = (P(None, "narrow", "wide", None), P())
    return jax.shard_map(
        on_device, mesh=mesh, in_specs=in_specs, out_specs=out_specs, check_vma=False
    )
```

```python
import functools

import jax
import jax.numpy as jnp
from jax import lax
from jax.experimental import pallas as pl
from jax.experimental.pallas import tpu as pltpu
from jax.sharding import PartitionSpec as P

RANK = 256
ROWS = 512
NZD, NXD, NCD, NYD = 8, 4, 2, 4
WIDE = NZD * NXD * NCD
CHUNKS = 8
MESH = pl.DeviceIdType.MESH
HIGHEST = lax.Precision.HIGHEST


def exchange_gram_kernel(
    x_ref, u_ref, g_ref,
    xin, stag, ubuf, gacc, r1, h2, r2, r3, gfull,
    in_sem, a_send, a_recv, out_sem, red_send, red_recv,
):
    w = lax.axis_index("wide")
    y = lax.axis_index("narrow")
    z, x, c = w // 8, (w // 2) % 4, w % 2
    piece = x * NYD + y

    def wide_id(zz, xx, cc):
        return zz * 8 + xx * 2 + cc

    barrier = pltpu.get_barrier_semaphore()

    def greet(i, carry):
        pl.semaphore_signal(barrier, inc=1, device_id=((w + i) % WIDE, y), device_id_type=MESH)
        return carry

    lax.fori_loop(1, WIDE, greet, 0)

    def greet_plane(i, carry):
        yy, xx = (y + 1 + i // NXD) % NYD, i % NXD
        pl.semaphore_signal(
            barrier, inc=1, device_id=(wide_id(z, xx, c), yy), device_id_type=MESH
        )
        return carry

    lax.fori_loop(0, (NYD - 1) * NXD, greet_plane, 0)

    def load(i, carry):
        yy, r = i // 8, i % 8
        pltpu.make_async_copy(
            x_ref.at[r, yy], xin.at[pl.ds(pl.multiple_of(i * 512, 512), 512)], in_sem.at[yy]
        ).start()
        return carry

    lax.fori_loop(0, 32, load, 0)

    def relayout(ch):
        yy, zh = ch // 2, ch % 2
        base = yy * 4096 + zh * 4

        def body(d, carry):
            for q in range(4):
                stag[ch, d, q] = xin[pl.ds(base + d * 8 + q, 8, stride=512), :]
            return carry

        lax.fori_loop(0, WIDE, body, 0, unroll=4)
        for q in range(4):
            ubuf[ch, q, w] = stag[ch, w, q]

    def wait_in(yy):
        whole = xin.at[pl.ds(pl.multiple_of(yy * 4096, 4096), 4096)]
        pltpu.make_async_copy(whole, whole, in_sem.at[yy]).wait()

    def send(ch):
        def body(i, carry):
            off = (i * 27) % WIDE
            t = wide_id((z + off // 8) % NZD, (x + (off // 2) % 4) % NXD, (c + off % 2) % NCD)
            pltpu.make_async_remote_copy(
                src_ref=stag.at[ch, t],
                dst_ref=ubuf.at[ch, :, w],
                send_sem=a_send.at[ch],
                recv_sem=a_recv.at[ch],
                device_id=(t, y),
                device_id_type=MESH,
            ).start()
            return carry

        lax.fori_loop(1, WIDE, body, 0)

    wait_in(0)
    relayout(0)
    pl.semaphore_wait(barrier, WIDE - 1 + (NYD - 1) * NXD)
    send(0)
    relayout(1)
    send(1)

    def send_two(yy, carry):
        wait_in(yy)
        for zh in range(2):
            relayout(yy * 2 + zh)
            send(yy * 2 + zh)
        return carry

    lax.fori_loop(1, 4, send_two, 0)

    gacc[...] = jnp.zeros_like(gacc)

    def gram(ch, carry):
        got = ubuf.at[ch, :, pl.ds(0, WIDE - 1)]
        pltpu.make_async_copy(got, got, a_recv.at[ch]).wait()
        pltpu.make_async_copy(ubuf.at[ch], u_ref.at[ch], out_sem.at[ch]).start()
        for q in range(0, 4, 2):
            left = ubuf[ch, q].reshape(ROWS, 128)
            right = ubuf[ch, q + 1].reshape(ROWS, 128)
            a = jnp.concatenate([left, right], axis=1)
            part = lax.dot_general(
                a[:RANK], a, (((1,), (1,)), ((), ())),
                precision=HIGHEST, preferred_element_type=jnp.float32,
            )
            gacc[...] += part.reshape(2, 16, 8, ROWS)
        return carry

    lax.fori_loop(0, CHUNKS, gram, 0)

    partner = wide_id(z, x, 1 - c)
    pltpu.make_async_remote_copy(
        src_ref=gacc.at[1 - c], dst_ref=r1, send_sem=red_send.at[0], recv_sem=red_recv.at[0],
        device_id=(partner, y), device_id_type=MESH,
    ).start()
    pltpu.make_async_copy(r1, r1, red_recv.at[0]).wait()
    h2[...] = gacc[c] + r1[...]

    def plane(i, stage, source, target):
        t = (piece + i) % 16
        pltpu.make_async_remote_copy(
            src_ref=source(t), dst_ref=target, send_sem=red_send.at[stage],
            recv_sem=red_recv.at[stage], device_id=(wide_id(z, t // NYD, c), t % NYD),
            device_id_type=MESH,
        ).start()

    def scatter(i, carry):
        plane(i, 1, lambda t: h2.at[t], r2.at[piece])
        return carry

    lax.fori_loop(1, 16, scatter, 0)
    r2[piece] = h2[piece]
    got = r2.at[pl.ds(0, 15)]
    pltpu.make_async_copy(got, got, red_recv.at[1]).wait()
    total = r2[0]
    for i in range(1, 16):
        total = total + r2[i]
    r3[z] = total

    def along_z(i, carry):
        zz = (z + i) % NZD
        pltpu.make_async_remote_copy(
            src_ref=r3.at[z], dst_ref=r3.at[z], send_sem=red_send.at[2],
            recv_sem=red_recv.at[2], device_id=(wide_id(zz, x, c), y), device_id_type=MESH,
        ).start()
        return carry

    lax.fori_loop(1, NZD, along_z, 0)
    got = r3.at[pl.ds(0, NZD - 1)]
    pltpu.make_async_copy(got, got, red_recv.at[2]).wait()
    total = r3[0]
    for i in range(1, NZD):
        total = total + r3[i]
    gfull[c, piece] = total

    def gather(i, carry):
        plane(i, 3, lambda t: gfull.at[c, piece], gfull.at[c, piece])
        return carry

    lax.fori_loop(1, 16, gather, 0)
    got = gfull.at[c, pl.ds(0, 15)]
    pltpu.make_async_copy(got, got, red_recv.at[3]).wait()
    pltpu.make_async_remote_copy(
        src_ref=gfull.at[c], dst_ref=gfull.at[c], send_sem=red_send.at[4],
        recv_sem=red_recv.at[4], device_id=(partner, y), device_id_type=MESH,
    ).start()
    pltpu.make_async_copy(gfull.at[0], gfull.at[0], red_recv.at[4]).wait()
    g_ref[...] = gfull[...].reshape(RANK, ROWS)

    def drain(ch, carry):
        sent = stag.at[ch, pl.ds(0, WIDE - 1)]
        pltpu.make_async_copy(sent, sent, a_send.at[ch]).wait()
        pltpu.make_async_copy(ubuf.at[ch], u_ref.at[ch], out_sem.at[ch]).wait()
        return carry

    lax.fori_loop(0, CHUNKS, drain, 0)
    pltpu.make_async_copy(r1, r1, red_send.at[0]).wait()
    sent = h2.at[pl.ds(0, 15)]
    pltpu.make_async_copy(sent, sent, red_send.at[1]).wait()
    sent = r3.at[pl.ds(0, NZD - 1)]
    pltpu.make_async_copy(sent, sent, red_send.at[2]).wait()
    sent = gfull.at[c, pl.ds(0, 15)]
    pltpu.make_async_copy(sent, sent, red_send.at[3]).wait()
    pltpu.make_async_copy(gfull.at[0], gfull.at[0], red_send.at[4]).wait()


def exchange_gram(snapshot):
    f32 = jnp.float32
    dma = pltpu.SemaphoreType.DMA
    return pl.pallas_call(
        exchange_gram_kernel,
        name="exchange_gram",
        out_shape=(
            jax.ShapeDtypeStruct((CHUNKS, 4, WIDE, 8, 128), f32),
            jax.ShapeDtypeStruct((RANK, ROWS), f32),
        ),
        in_specs=[pl.BlockSpec(memory_space=pl.ANY)],
        out_specs=(
            pl.BlockSpec(memory_space=pl.ANY),
            pl.BlockSpec(memory_space=pltpu.VMEM),
        ),
        scratch_shapes=[
            pltpu.VMEM((4 * 8 * 512, 128), f32),
            pltpu.VMEM((CHUNKS, WIDE, 4, 8, 128), f32),
            pltpu.VMEM((CHUNKS, 4, WIDE, 8, 128), f32),
            pltpu.VMEM((2, 16, 8, ROWS), f32),
            pltpu.VMEM((16, 8, ROWS), f32),
            pltpu.VMEM((16, 8, ROWS), f32),
            pltpu.VMEM((16, 8, ROWS), f32),
            pltpu.VMEM((NZD, 8, ROWS), f32),
            pltpu.VMEM((2, 16, 8, ROWS), f32),
            dma((4,)), dma((CHUNKS,)), dma((CHUNKS,)), dma((CHUNKS,)), dma((5,)), dma((5,)),
        ],
        compiler_params=pltpu.CompilerParams(
            collective_id=0, has_side_effects=True, vmem_limit_bytes=48 << 20
        ),
    )(snapshot)


def tree(terms):
    while len(terms) > 1:
        terms = [sum(terms[i + 1 : i + 2], terms[i]) for i in range(0, len(terms), 2)]
    return terms[0]


def unit_lower_inverse(rows, tmp):
    tile = (8, 128)
    lane = lax.broadcasted_iota(jnp.int32, tile, 1)
    sub = lax.broadcasted_iota(jnp.int32, tile, 0)
    rows, done = list(rows), []

    def lanes(v, k):
        return jnp.broadcast_to(v[:, k : k + 1], tile)

    def subs(v, k):
        return jnp.broadcast_to(v[k : k + 1, :], tile)

    for g in range(16):
        v = rows[g]
        inside = (lane >= 8 * g) & (lane < 8 * g + 8)
        cols = [lanes(v, 8 * g + k) for k in range(8)]
        base = 256 * (g % 2)
        for k in range(8):
            tmp[base + 8 * k : base + 8 * k + 8, :] = cols[k]
        def row(r):
            return tmp[pl.ds(base + r, 8, stride=0), :]
        a = [[row(8 * k + i) if i >= k else None for k in range(8)] for i in range(8)]
        n = [[None] * 8 for _ in range(8)]
        m = [[None] * 8 for _ in range(8)]
        inv = [None] * 8
        for k in range(8):
            inv[k] = 1.0 / a[k][k]
            for i in range(k + 1, 8):
                m[i][k] = a[i][k] * inv[k]
                for j in range(k + 1, i + 1):
                    a[i][j] = a[i][j] - m[i][k] * a[j][k]
        for j in range(8):
            for i in range(j + 1, 8):
                s = m[i][j]
                for t in range(j + 1, i):
                    s = s + m[i][t] * n[t][j]
                n[i][j] = -s
        vt = jnp.where(inside, jnp.where(lane == 8 * g + sub, 1.0, 0.0), v)
        tmp[base + 64 : base + 72, :] = vt
        terms = [vt]
        for k in range(7):
            col = jnp.zeros(tile, jnp.float32)
            for i in range(k + 1, 8):
                col = jnp.where(sub == i, n[i][k], col)
            terms.append(col * row(64 + k))
        p = tree(terms)
        scale = inv[0]
        for i in range(1, 8):
            scale = jnp.where(sub == i, inv[i], scale)
        q = p * scale
        tmp[base + 72 : base + 80, :] = q
        qb = [row(72 + i) for i in range(8)]
        tb = []
        for j in range(8):
            tb.append(tree([qb[j]] + [n[i][j] * qb[i] for i in range(j + 1, 8)]))
        done.append(jnp.where(lane < 8 * g + 8, p, 0.0))
        for i in range(g + 1, 16):
            vi = rows[i]
            c = [lanes(vi, 8 * g + k) for k in range(8)]
            vi = jnp.where(inside, 0.0, vi)
            rows[i] = vi - tree([c[k] * tb[k] for k in range(8)])
    return done


def eliminate(a, tmp):
    n = a.shape[1]
    inv = jnp.concatenate(unit_lower_inverse([a[8 * g : 8 * g + 8, :128] for g in range(16)], tmp), axis=0)
    s = jnp.dot(inv, a, precision=HIGHEST, preferred_element_type=jnp.float32)
    row = lax.broadcasted_iota(jnp.int32, (128, n), 0)
    lane = lax.broadcasted_iota(jnp.int32, (128, n), 1)
    s = jnp.where(lane >= row, s, 0.0)
    d = jnp.sum(jnp.where(lane[:, :128] == row[:, :128], s[:, :128], 0.0), axis=1, keepdims=True)
    return s, d


def unit_rows(s, d):
    r = s * (1.0 / jnp.sqrt(d))
    return r * (1.0 / jnp.sqrt(jnp.sum(r * r, axis=1, keepdims=True)))


def factor_rows(g_ref, ft_ref, tmp):
    s1, d1 = eliminate(g_ref[:128, :], tmp)
    ft_ref[:128, :] = unit_rows(s1, d1)
    right = s1[:, 128:]
    schur = lax.dot_general(right[:, :128] * (1.0 / d1), right, (((0,), (0,)), ((), ())),
        precision=HIGHEST, preferred_element_type=jnp.float32)
    s2, d2 = eliminate(g_ref[128:, 128:] - schur, tmp)
    ft_ref[128:, :128] = jnp.zeros((128, 128), jnp.float32)
    ft_ref[128:, 128:] = unit_rows(s2, d2)


def split(v):
    high = v.astype(jnp.bfloat16)
    return high, (v - high.astype(jnp.float32)).astype(jnp.bfloat16)


def core_kernel(u_ref, g_ref, core_ref, factor_ref, ubuf, cbuf, ft, tmp, in_sem, out_sem):
    def begin(ch, carry):
        pltpu.make_async_copy(u_ref.at[ch], ubuf.at[ch], in_sem.at[ch]).start()
        return carry

    lax.fori_loop(0, CHUNKS, begin, 0)
    factor_rows(g_ref, ft, tmp)
    high, low = split(ft[...])
    dot = functools.partial(jnp.dot, preferred_element_type=jnp.float32)
    flat = cbuf.reshape(NYD * RANK * 8, 128)

    def end(ch, carry):
        pltpu.make_async_copy(u_ref.at[ch], ubuf.at[ch], in_sem.at[ch]).wait()
        return carry

    lax.fori_loop(0, CHUNKS, end, 0)
    for y in range(NYD):
        for zz in range(0, 8, 2):
            cells = [ubuf[2 * y + (zz + k) // 4, (zz + k) % 4].reshape(ROWS, 128) for k in range(2)]
            ah, al = split(jnp.concatenate(cells, axis=1))
            out = dot(high, ah) + (dot(high, al) + dot(low, ah))
            for k in range(2):
                start = y * RANK * 8 + zz + k
                flat[pl.ds(start, RANK, stride=8), :] = out[:, 128 * k : 128 * k + 128]
        pltpu.make_async_copy(cbuf.at[y], core_ref.at[:, y], out_sem.at[y]).start()
        factor_ref[128 * y : 128 * y + 128, :] = ft[:, 128 * y : 128 * y + 128].T
    for y in range(NYD):
        pltpu.make_async_copy(cbuf.at[y], core_ref.at[:, y], out_sem.at[y]).wait()


def project(u, gram):
    f32 = jnp.float32
    return pl.pallas_call(
        core_kernel,
        name="project",
        out_shape=(
            jax.ShapeDtypeStruct((RANK, NYD, 8, 128), f32),
            jax.ShapeDtypeStruct((ROWS, RANK), f32),
        ),
        in_specs=[pl.BlockSpec(memory_space=pl.ANY), pl.BlockSpec(memory_space=pltpu.VMEM)],
        out_specs=(pl.BlockSpec(memory_space=pl.ANY), pl.BlockSpec(memory_space=pltpu.VMEM)),
        scratch_shapes=[
            pltpu.VMEM((CHUNKS, 4, WIDE, 8, 128), f32),
            pltpu.VMEM((NYD, RANK, 8, 128), f32),
            pltpu.VMEM((RANK, ROWS), f32),
            pltpu.VMEM((512, 128), f32),
            pltpu.SemaphoreType.DMA((CHUNKS,)),
            pltpu.SemaphoreType.DMA((NYD,)),
        ],
        compiler_params=pltpu.CompilerParams(vmem_limit_bytes=48 << 20),
    )(u, gram)


def on_device(snapshot):
    u, gram = exchange_gram(snapshot)
    return project(u, gram)


def solution(mesh):
    in_specs = (P("wide", "narrow", None, None),)
    out_specs = (P(None, "narrow", "wide", None), P())
    return jax.shard_map(
        on_device, mesh=mesh, in_specs=in_specs, out_specs=out_specs, check_vma=False
    )
```

```python
import functools

import jax
import jax.numpy as jnp
from jax import lax
from jax.experimental import pallas as pl
from jax.experimental.pallas import tpu as pltpu
from jax.sharding import PartitionSpec as P

RANK = 256
ROWS = 512
NZD, NXD, NCD, NYD = 8, 4, 2, 4
WIDE = NZD * NXD * NCD
CHUNKS = 8
PLANE = (
    (2, 2), (2, 1), (2, 3), (1, 2), (3, 2), (1, 1), (1, 3), (3, 1),
    (3, 3), (0, 2), (2, 0), (0, 1), (0, 3), (1, 0), (3, 0),
)
MESH = pl.DeviceIdType.MESH
HIGHEST = lax.Precision.HIGHEST


def split(v):
    high = v.astype(jnp.bfloat16)
    return high, (v - high.astype(jnp.float32)).astype(jnp.bfloat16)


def exchange_gram_kernel(
    x_ref, uh_ref, ul_ref, g_ref,
    xin, stag, ubuf, uh, ul, gacc, r1, h2, r2, r3, gfull,
    in_sem, a_send, a_recv, out_sem, red_send, red_recv, piece_recv,
):
    w = lax.axis_index("wide")
    y = lax.axis_index("narrow")
    z, x, c = w // 8, (w // 2) % 4, w % 2
    piece = x * NYD + y

    def wide_id(zz, xx, cc):
        return zz * 8 + xx * 2 + cc

    barrier = pltpu.get_barrier_semaphore()

    def greet(i, carry):
        pl.semaphore_signal(barrier, inc=1, device_id=((w + i) % WIDE, y), device_id_type=MESH)
        return carry

    lax.fori_loop(1, WIDE, greet, 0)

    def greet_plane(i, carry):
        yy, xx = (y + 1 + i // NXD) % NYD, i % NXD
        pl.semaphore_signal(
            barrier, inc=1, device_id=(wide_id(z, xx, c), yy), device_id_type=MESH
        )
        return carry

    lax.fori_loop(0, (NYD - 1) * NXD, greet_plane, 0)

    def load(i, carry):
        yy, r = i // 8, i % 8
        pltpu.make_async_copy(
            x_ref.at[r, yy], xin.at[pl.ds(pl.multiple_of(i * 512, 512), 512)], in_sem.at[yy]
        ).start()
        return carry

    lax.fori_loop(0, 32, load, 0)

    def relayout(ch):
        yy, zh = ch // 2, ch % 2
        base = yy * 4096 + zh * 4

        def body(d, carry):
            for q in range(4):
                stag[ch, d, q] = xin[pl.ds(base + d * 8 + q, 8, stride=512), :]
            return carry

        lax.fori_loop(0, WIDE, body, 0, unroll=4)
        for q in range(4):
            ubuf[ch, q, w] = stag[ch, w, q]

    def wait_in(yy):
        whole = xin.at[pl.ds(pl.multiple_of(yy * 4096, 4096), 4096)]
        pltpu.make_async_copy(whole, whole, in_sem.at[yy]).wait()

    def send(ch):
        def body(i, carry):
            off = (i * 27) % WIDE
            t = wide_id((z + off // 8) % NZD, (x + (off // 2) % 4) % NXD, (c + off % 2) % NCD)
            pltpu.make_async_remote_copy(
                src_ref=stag.at[ch, t],
                dst_ref=ubuf.at[ch, :, w],
                send_sem=a_send.at[ch],
                recv_sem=a_recv.at[ch],
                device_id=(t, y),
                device_id_type=MESH,
            ).start()
            return carry

        lax.fori_loop(1, WIDE, body, 0)

    wait_in(0)
    relayout(0)
    pl.semaphore_wait(barrier, WIDE - 1 + (NYD - 1) * NXD)
    send(0)
    relayout(1)
    send(1)

    def send_two(yy, carry):
        wait_in(yy)
        for zh in range(2):
            relayout(yy * 2 + zh)
            send(yy * 2 + zh)
        return carry

    lax.fori_loop(1, 4, send_two, 0)

    gacc[...] = jnp.zeros_like(gacc)

    def gram(ch, carry):
        got = ubuf.at[ch, :, pl.ds(0, WIDE - 1)]
        pltpu.make_async_copy(got, got, a_recv.at[ch]).wait()
        for q in range(0, 4, 2):
            left = ubuf[ch, q].reshape(ROWS, 128)
            right = ubuf[ch, q + 1].reshape(ROWS, 128)
            a = jnp.concatenate([left, right], axis=1)
            part = lax.dot_general(
                a[:RANK], a, (((1,), (1,)), ((), ())),
                precision=HIGHEST, preferred_element_type=jnp.float32,
            )
            gacc[...] += part.reshape(2, 16, 8, ROWS)
            high, low = split(a)
            for k in range(2):
                uh[ch, q + k] = high[:, 128 * k : 128 * k + 128]
                ul[ch, q + k] = low[:, 128 * k : 128 * k + 128]
        pltpu.make_async_copy(uh.at[ch], uh_ref.at[ch], out_sem.at[0, ch]).start()
        pltpu.make_async_copy(ul.at[ch], ul_ref.at[ch], out_sem.at[1, ch]).start()
        return carry

    lax.fori_loop(0, CHUNKS, gram, 0)

    partner = wide_id(z, x, 1 - c)
    pltpu.make_async_remote_copy(
        src_ref=gacc.at[1 - c], dst_ref=r1, send_sem=red_send.at[0], recv_sem=red_recv.at[0],
        device_id=(partner, y), device_id_type=MESH,
    ).start()
    pltpu.make_async_copy(r1, r1, red_recv.at[0]).wait()
    h2[...] = gacc[c] + r1[...]

    for dx, dy in PLANE:
        xx, yy = (x + dx) % NXD, (y + dy) % NYD
        pltpu.make_async_remote_copy(
            src_ref=h2.at[xx * NYD + yy], dst_ref=r2.at[piece], send_sem=red_send.at[1],
            recv_sem=red_recv.at[1], device_id=(wide_id(z, xx, c), yy), device_id_type=MESH,
        ).start()
    r2[piece] = h2[piece]
    got = r2.at[pl.ds(0, 15)]
    pltpu.make_async_copy(got, got, red_recv.at[1]).wait()
    total = r2[0]
    for i in range(1, 16):
        total = total + r2[i]
    r3[z] = total

    def along_z(i, carry):
        zz = (z + i) % NZD
        pltpu.make_async_remote_copy(
            src_ref=r3.at[z], dst_ref=r3.at[z], send_sem=red_send.at[2],
            recv_sem=red_recv.at[2], device_id=(wide_id(zz, x, c), y), device_id_type=MESH,
        ).start()
        return carry

    lax.fori_loop(1, NZD, along_z, 0)
    got = r3.at[pl.ds(0, NZD - 1)]
    pltpu.make_async_copy(got, got, red_recv.at[2]).wait()
    total = r3[0]
    for i in range(1, NZD):
        total = total + r3[i]
    gfull[c, piece] = total

    def across(p):
        pltpu.make_async_remote_copy(
            src_ref=gfull.at[c, p], dst_ref=gfull.at[c, p], send_sem=red_send.at[4],
            recv_sem=red_recv.at[3], device_id=(partner, y), device_id_type=MESH,
        ).start()

    for dx, dy in PLANE:
        xx, yy = (x + dx) % NXD, (y + dy) % NYD
        pltpu.make_async_remote_copy(
            src_ref=gfull.at[c, piece], dst_ref=gfull.at[c, piece], send_sem=red_send.at[3],
            recv_sem=piece_recv.at[piece], device_id=(wide_id(z, xx, c), yy), device_id_type=MESH,
        ).start()
    across(piece)
    for dx, dy in PLANE[::-1]:
        p = ((x + NXD - dx) % NXD) * NYD + (y + NYD - dy) % NYD
        pltpu.make_async_copy(gfull.at[c, p], gfull.at[c, p], piece_recv.at[p]).wait()
        across(p)
    pltpu.make_async_copy(gfull.at[0], gfull.at[0], red_recv.at[3]).wait()
    g_ref[...] = gfull[...].reshape(RANK, ROWS)

    def drain(ch, carry):
        sent = stag.at[ch, pl.ds(0, WIDE - 1)]
        pltpu.make_async_copy(sent, sent, a_send.at[ch]).wait()
        pltpu.make_async_copy(uh.at[ch], uh_ref.at[ch], out_sem.at[0, ch]).wait()
        pltpu.make_async_copy(ul.at[ch], ul_ref.at[ch], out_sem.at[1, ch]).wait()
        return carry

    lax.fori_loop(0, CHUNKS, drain, 0)
    pltpu.make_async_copy(r1, r1, red_send.at[0]).wait()
    sent = h2.at[pl.ds(0, 15)]
    pltpu.make_async_copy(sent, sent, red_send.at[1]).wait()
    sent = r3.at[pl.ds(0, NZD - 1)]
    pltpu.make_async_copy(sent, sent, red_send.at[2]).wait()
    sent = gfull.at[c, pl.ds(0, 15)]
    pltpu.make_async_copy(sent, sent, red_send.at[3]).wait()
    pltpu.make_async_copy(gfull.at[0], gfull.at[0], red_send.at[4]).wait()


def exchange_gram(snapshot):
    f32 = jnp.float32
    dma = pltpu.SemaphoreType.DMA
    return pl.pallas_call(
        exchange_gram_kernel,
        name="exchange_gram",
        out_shape=(
            jax.ShapeDtypeStruct((CHUNKS, 4, ROWS, 128), jnp.bfloat16),
            jax.ShapeDtypeStruct((CHUNKS, 4, ROWS, 128), jnp.bfloat16),
            jax.ShapeDtypeStruct((RANK, ROWS), f32),
        ),
        in_specs=[pl.BlockSpec(memory_space=pl.ANY)],
        out_specs=(
            pl.BlockSpec(memory_space=pl.ANY),
            pl.BlockSpec(memory_space=pl.ANY),
            pl.BlockSpec(memory_space=pltpu.VMEM),
        ),
        scratch_shapes=[
            pltpu.VMEM((4 * 8 * 512, 128), f32),
            pltpu.VMEM((CHUNKS, WIDE, 4, 8, 128), f32),
            pltpu.VMEM((CHUNKS, 4, WIDE, 8, 128), f32),
            pltpu.VMEM((CHUNKS, 4, ROWS, 128), jnp.bfloat16),
            pltpu.VMEM((CHUNKS, 4, ROWS, 128), jnp.bfloat16),
            pltpu.VMEM((2, 16, 8, ROWS), f32),
            pltpu.VMEM((16, 8, ROWS), f32),
            pltpu.VMEM((16, 8, ROWS), f32),
            pltpu.VMEM((16, 8, ROWS), f32),
            pltpu.VMEM((NZD, 8, ROWS), f32),
            pltpu.VMEM((2, 16, 8, ROWS), f32),
            dma((4,)), dma((CHUNKS,)), dma((CHUNKS,)), dma((2, CHUNKS)), dma((5,)), dma((4,)), dma((16,)),
        ],
        compiler_params=pltpu.CompilerParams(
            collective_id=0, has_side_effects=True, vmem_limit_bytes=48 << 20
        ),
    )(snapshot)


def tree(terms):
    while len(terms) > 1:
        terms = [sum(terms[i + 1 : i + 2], terms[i]) for i in range(0, len(terms), 2)]
    return terms[0]


def unit_lower_inverse(rows, tmp):
    tile = (8, 128)
    lane = lax.broadcasted_iota(jnp.int32, tile, 1)
    sub = lax.broadcasted_iota(jnp.int32, tile, 0)
    rows, done = list(rows), []

    def lanes(v, k):
        return jnp.broadcast_to(v[:, k : k + 1], tile)

    def subs(v, k):
        return jnp.broadcast_to(v[k : k + 1, :], tile)

    for g in range(16):
        v = rows[g]
        inside = (lane >= 8 * g) & (lane < 8 * g + 8)
        cols = [lanes(v, 8 * g + k) for k in range(8)]
        base = 256 * (g % 2)
        for k in range(8):
            tmp[base + 8 * k : base + 8 * k + 8, :] = cols[k]
        def row(r):
            return tmp[pl.ds(base + r, 8, stride=0), :]
        a = [[row(8 * k + i) if i >= k else None for k in range(8)] for i in range(8)]
        n = [[None] * 8 for _ in range(8)]
        m = [[None] * 8 for _ in range(8)]
        inv = [None] * 8
        for k in range(8):
            inv[k] = 1.0 / a[k][k]
            for i in range(k + 1, 8):
                m[i][k] = a[i][k] * inv[k]
                for j in range(k + 1, i + 1):
                    a[i][j] = a[i][j] - m[i][k] * a[j][k]
        for j in range(8):
            for i in range(j + 1, 8):
                s = m[i][j]
                for t in range(j + 1, i):
                    s = s + m[i][t] * n[t][j]
                n[i][j] = -s
        vt = jnp.where(inside, jnp.where(lane == 8 * g + sub, 1.0, 0.0), v)
        tmp[base + 64 : base + 72, :] = vt
        terms = [vt]
        for k in range(7):
            col = jnp.zeros(tile, jnp.float32)
            for i in range(k + 1, 8):
                col = jnp.where(sub == i, n[i][k], col)
            terms.append(col * row(64 + k))
        p = tree(terms)
        scale = inv[0]
        for i in range(1, 8):
            scale = jnp.where(sub == i, inv[i], scale)
        q = p * scale
        tmp[base + 72 : base + 80, :] = q
        qb = [row(72 + i) for i in range(8)]
        tb = []
        for j in range(8):
            tb.append(tree([qb[j]] + [n[i][j] * qb[i] for i in range(j + 1, 8)]))
        done.append(jnp.where(lane < 8 * g + 8, p, 0.0))
        for i in range(g + 1, 16):
            vi = rows[i]
            c = [lanes(vi, 8 * g + k) for k in range(8)]
            vi = jnp.where(inside, 0.0, vi)
            rows[i] = vi - tree([c[k] * tb[k] for k in range(8)])
    return done


def eliminate(a, tmp):
    n = a.shape[1]
    inv = jnp.concatenate(unit_lower_inverse([a[8 * g : 8 * g + 8, :128] for g in range(16)], tmp), axis=0)
    s = jnp.dot(inv, a, precision=HIGHEST, preferred_element_type=jnp.float32)
    row = lax.broadcasted_iota(jnp.int32, (128, n), 0)
    lane = lax.broadcasted_iota(jnp.int32, (128, n), 1)
    s = jnp.where(lane >= row, s, 0.0)
    d = jnp.sum(jnp.where(lane[:, :128] == row[:, :128], s[:, :128], 0.0), axis=1, keepdims=True)
    return s, d


def unit_rows(s, d):
    r = s * (1.0 / jnp.sqrt(d))
    return r * (1.0 / jnp.sqrt(jnp.sum(r * r, axis=1, keepdims=True)))


def factor_rows(g_ref, ft_ref, tmp):
    s1, d1 = eliminate(g_ref[:128, :], tmp)
    ft_ref[:128, :] = unit_rows(s1, d1)
    right = s1[:, 128:]
    schur = lax.dot_general(right[:, :128] * (1.0 / d1), right, (((0,), (0,)), ((), ())),
        precision=HIGHEST, preferred_element_type=jnp.float32)
    s2, d2 = eliminate(g_ref[128:, 128:] - schur, tmp)
    ft_ref[128:, :128] = jnp.zeros((128, 128), jnp.float32)
    ft_ref[128:, 128:] = unit_rows(s2, d2)


def core_kernel(
    uh_ref, ul_ref, g_ref, core_ref, factor_ref, uh, ul, cbuf, ft, tmp, in_sem, out_sem
):
    def begin(ch, carry):
        pltpu.make_async_copy(uh_ref.at[ch], uh.at[ch], in_sem.at[0, ch]).start()
        pltpu.make_async_copy(ul_ref.at[ch], ul.at[ch], in_sem.at[1, ch]).start()
        return carry

    lax.fori_loop(0, CHUNKS, begin, 0)
    factor_rows(g_ref, ft, tmp)
    high, low = split(ft[...])
    dot = functools.partial(jnp.dot, preferred_element_type=jnp.float32)
    flat = cbuf.reshape(NYD * RANK * 8, 128)

    def end(ch, carry):
        pltpu.make_async_copy(uh_ref.at[ch], uh.at[ch], in_sem.at[0, ch]).wait()
        pltpu.make_async_copy(ul_ref.at[ch], ul.at[ch], in_sem.at[1, ch]).wait()
        return carry

    lax.fori_loop(0, CHUNKS, end, 0)
    for y in range(NYD):
        for zz in range(0, 8, 2):
            ch, q = 2 * y + zz // 4, zz % 4
            ah = jnp.concatenate([uh[ch, q], uh[ch, q + 1]], axis=1)
            al = jnp.concatenate([ul[ch, q], ul[ch, q + 1]], axis=1)
            out = dot(high, ah) + (dot(high, al) + dot(low, ah))
            for k in range(2):
                start = y * RANK * 8 + zz + k
                flat[pl.ds(start, RANK, stride=8), :] = out[:, 128 * k : 128 * k + 128]
        pltpu.make_async_copy(cbuf.at[y], core_ref.at[:, y], out_sem.at[y]).start()
        factor_ref[128 * y : 128 * y + 128, :] = ft[:, 128 * y : 128 * y + 128].T
    for y in range(NYD):
        pltpu.make_async_copy(cbuf.at[y], core_ref.at[:, y], out_sem.at[y]).wait()


def project(uh, ul, gram):
    f32 = jnp.float32
    return pl.pallas_call(
        core_kernel,
        name="project",
        out_shape=(
            jax.ShapeDtypeStruct((RANK, NYD, 8, 128), f32),
            jax.ShapeDtypeStruct((ROWS, RANK), f32),
        ),
        in_specs=[
            pl.BlockSpec(memory_space=pl.ANY),
            pl.BlockSpec(memory_space=pl.ANY),
            pl.BlockSpec(memory_space=pltpu.VMEM),
        ],
        out_specs=(pl.BlockSpec(memory_space=pl.ANY), pl.BlockSpec(memory_space=pltpu.VMEM)),
        scratch_shapes=[
            pltpu.VMEM((CHUNKS, 4, ROWS, 128), jnp.bfloat16),
            pltpu.VMEM((CHUNKS, 4, ROWS, 128), jnp.bfloat16),
            pltpu.VMEM((NYD, RANK, 8, 128), f32),
            pltpu.VMEM((RANK, ROWS), f32),
            pltpu.VMEM((512, 128), f32),
            pltpu.SemaphoreType.DMA((2, CHUNKS)),
            pltpu.SemaphoreType.DMA((NYD,)),
        ],
        compiler_params=pltpu.CompilerParams(vmem_limit_bytes=48 << 20),
    )(uh, ul, gram)


def on_device(snapshot):
    uh, ul, gram = exchange_gram(snapshot)
    return project(uh, ul, gram)


def solution(mesh):
    in_specs = (P("wide", "narrow", None, None),)
    out_specs = (P(None, "narrow", "wide", None), P())
    return jax.shard_map(
        on_device, mesh=mesh, in_specs=in_specs, out_specs=out_specs, check_vma=False
    )
```

```python
import functools

import jax
import jax.numpy as jnp
from jax import lax
from jax.experimental import pallas as pl
from jax.experimental.pallas import tpu as pltpu
from jax.sharding import PartitionSpec as P

RANK = 256
ROWS = 512
NZD, NXD, NCD, NYD = 8, 4, 2, 4
WIDE = NZD * NXD * NCD
CHUNKS = 8
PLANE = (
    (2, 2), (2, 1), (2, 3), (1, 2), (3, 2), (1, 1), (1, 3), (3, 1),
    (3, 3), (0, 2), (2, 0), (0, 1), (0, 3), (1, 0), (3, 0),
)
MESH = pl.DeviceIdType.MESH
HIGHEST = lax.Precision.HIGHEST


def exchange_gram_kernel(
    x_ref, u_ref, g_ref,
    xin, stag, ubuf, gacc, r1, h2, r2, r3, gfull,
    in_sem, a_send, a_recv, out_sem, red_send, red_recv, piece_recv,
):
    w = lax.axis_index("wide")
    y = lax.axis_index("narrow")
    z, x, c = w // 8, (w // 2) % 4, w % 2
    piece = x * NYD + y

    def wide_id(zz, xx, cc):
        return zz * 8 + xx * 2 + cc

    barrier = pltpu.get_barrier_semaphore()

    def greet(i, carry):
        pl.semaphore_signal(barrier, inc=1, device_id=((w + i) % WIDE, y), device_id_type=MESH)
        return carry

    lax.fori_loop(1, WIDE, greet, 0)

    def greet_plane(i, carry):
        yy, xx = (y + 1 + i // NXD) % NYD, i % NXD
        pl.semaphore_signal(
            barrier, inc=1, device_id=(wide_id(z, xx, c), yy), device_id_type=MESH
        )
        return carry

    lax.fori_loop(0, (NYD - 1) * NXD, greet_plane, 0)

    def load(i, carry):
        yy, r = i // 8, i % 8
        pltpu.make_async_copy(
            x_ref.at[r, yy], xin.at[pl.ds(pl.multiple_of(i * 512, 512), 512)], in_sem.at[yy]
        ).start()
        return carry

    lax.fori_loop(0, 32, load, 0)

    def relayout(ch):
        yy, zh = ch // 2, ch % 2
        base = yy * 4096 + zh * 4

        def body(d, carry):
            for q in range(4):
                stag[ch, d, q] = xin[pl.ds(base + d * 8 + q, 8, stride=512), :]
            return carry

        lax.fori_loop(0, WIDE, body, 0, unroll=4)
        for q in range(4):
            ubuf[ch, q, w] = stag[ch, w, q]

    def wait_in(yy):
        whole = xin.at[pl.ds(pl.multiple_of(yy * 4096, 4096), 4096)]
        pltpu.make_async_copy(whole, whole, in_sem.at[yy]).wait()

    def send(ch):
        def body(i, carry):
            off = (i * 27) % WIDE
            t = wide_id((z + off // 8) % NZD, (x + (off // 2) % 4) % NXD, (c + off % 2) % NCD)
            pltpu.make_async_remote_copy(
                src_ref=stag.at[ch, t],
                dst_ref=ubuf.at[ch, :, w],
                send_sem=a_send.at[ch],
                recv_sem=a_recv.at[ch],
                device_id=(t, y),
                device_id_type=MESH,
            ).start()
            return carry

        lax.fori_loop(1, WIDE, body, 0)

    wait_in(0)
    relayout(0)
    pl.semaphore_wait(barrier, WIDE - 1 + (NYD - 1) * NXD)
    send(0)
    relayout(1)
    send(1)

    def send_two(yy, carry):
        wait_in(yy)
        for zh in range(2):
            relayout(yy * 2 + zh)
            send(yy * 2 + zh)
        return carry

    lax.fori_loop(1, 4, send_two, 0)

    gacc[...] = jnp.zeros_like(gacc)

    def gram(ch, carry):
        got = ubuf.at[ch, :, pl.ds(0, WIDE - 1)]
        pltpu.make_async_copy(got, got, a_recv.at[ch]).wait()
        pltpu.make_async_copy(ubuf.at[ch], u_ref.at[ch], out_sem.at[ch]).start()
        for q in range(0, 4, 2):
            left = ubuf[ch, q].reshape(ROWS, 128)
            right = ubuf[ch, q + 1].reshape(ROWS, 128)
            a = jnp.concatenate([left, right], axis=1)
            part = lax.dot_general(
                a[:RANK], a, (((1,), (1,)), ((), ())),
                precision=HIGHEST, preferred_element_type=jnp.float32,
            )
            gacc[...] += part.reshape(2, 16, 8, ROWS)
        return carry

    lax.fori_loop(0, CHUNKS, gram, 0)

    partner = wide_id(z, x, 1 - c)
    pltpu.make_async_remote_copy(
        src_ref=gacc.at[1 - c], dst_ref=r1, send_sem=red_send.at[0], recv_sem=red_recv.at[0],
        device_id=(partner, y), device_id_type=MESH,
    ).start()
    pltpu.make_async_copy(r1, r1, red_recv.at[0]).wait()
    h2[...] = gacc[c] + r1[...]

    for dx, dy in PLANE:
        xx, yy = (x + dx) % NXD, (y + dy) % NYD
        pltpu.make_async_remote_copy(
            src_ref=h2.at[xx * NYD + yy], dst_ref=r2.at[piece], send_sem=red_send.at[1],
            recv_sem=red_recv.at[1], device_id=(wide_id(z, xx, c), yy), device_id_type=MESH,
        ).start()
    r2[piece] = h2[piece]
    got = r2.at[pl.ds(0, 15)]
    pltpu.make_async_copy(got, got, red_recv.at[1]).wait()
    total = r2[0]
    for i in range(1, 16):
        total = total + r2[i]
    r3[z] = total

    def along_z(i, carry):
        zz = (z + i) % NZD
        pltpu.make_async_remote_copy(
            src_ref=r3.at[z], dst_ref=r3.at[z], send_sem=red_send.at[2],
            recv_sem=red_recv.at[2], device_id=(wide_id(zz, x, c), y), device_id_type=MESH,
        ).start()
        return carry

    lax.fori_loop(1, NZD, along_z, 0)
    got = r3.at[pl.ds(0, NZD - 1)]
    pltpu.make_async_copy(got, got, red_recv.at[2]).wait()
    total = r3[0]
    for i in range(1, NZD):
        total = total + r3[i]
    gfull[c, piece] = total

    def across(p):
        pltpu.make_async_remote_copy(
            src_ref=gfull.at[c, p], dst_ref=gfull.at[c, p], send_sem=red_send.at[4],
            recv_sem=red_recv.at[3], device_id=(partner, y), device_id_type=MESH,
        ).start()

    for dx, dy in PLANE:
        xx, yy = (x + dx) % NXD, (y + dy) % NYD
        pltpu.make_async_remote_copy(
            src_ref=gfull.at[c, piece], dst_ref=gfull.at[c, piece], send_sem=red_send.at[3],
            recv_sem=piece_recv.at[piece], device_id=(wide_id(z, xx, c), yy), device_id_type=MESH,
        ).start()
    across(piece)
    for dx, dy in PLANE[::-1]:
        p = ((x + NXD - dx) % NXD) * NYD + (y + NYD - dy) % NYD
        pltpu.make_async_copy(gfull.at[c, p], gfull.at[c, p], piece_recv.at[p]).wait()
        across(p)
    pltpu.make_async_copy(gfull.at[0], gfull.at[0], red_recv.at[3]).wait()
    g_ref[...] = gfull[...].reshape(RANK, ROWS)

    def drain(ch, carry):
        sent = stag.at[ch, pl.ds(0, WIDE - 1)]
        pltpu.make_async_copy(sent, sent, a_send.at[ch]).wait()
        pltpu.make_async_copy(ubuf.at[ch], u_ref.at[ch], out_sem.at[ch]).wait()
        return carry

    lax.fori_loop(0, CHUNKS, drain, 0)
    pltpu.make_async_copy(r1, r1, red_send.at[0]).wait()
    sent = h2.at[pl.ds(0, 15)]
    pltpu.make_async_copy(sent, sent, red_send.at[1]).wait()
    sent = r3.at[pl.ds(0, NZD - 1)]
    pltpu.make_async_copy(sent, sent, red_send.at[2]).wait()
    sent = gfull.at[c, pl.ds(0, 15)]
    pltpu.make_async_copy(sent, sent, red_send.at[3]).wait()
    pltpu.make_async_copy(gfull.at[0], gfull.at[0], red_send.at[4]).wait()


def exchange_gram(snapshot):
    f32 = jnp.float32
    dma = pltpu.SemaphoreType.DMA
    return pl.pallas_call(
        exchange_gram_kernel,
        name="exchange_gram",
        out_shape=(
            jax.ShapeDtypeStruct((CHUNKS, 4, WIDE, 8, 128), f32),
            jax.ShapeDtypeStruct((RANK, ROWS), f32),
        ),
        in_specs=[pl.BlockSpec(memory_space=pl.ANY)],
        out_specs=(
            pl.BlockSpec(memory_space=pl.ANY),
            pl.BlockSpec(memory_space=pltpu.VMEM),
        ),
        scratch_shapes=[
            pltpu.VMEM((4 * 8 * 512, 128), f32),
            pltpu.VMEM((CHUNKS, WIDE, 4, 8, 128), f32),
            pltpu.VMEM((CHUNKS, 4, WIDE, 8, 128), f32),
            pltpu.VMEM((2, 16, 8, ROWS), f32),
            pltpu.VMEM((16, 8, ROWS), f32),
            pltpu.VMEM((16, 8, ROWS), f32),
            pltpu.VMEM((16, 8, ROWS), f32),
            pltpu.VMEM((NZD, 8, ROWS), f32),
            pltpu.VMEM((2, 16, 8, ROWS), f32),
            dma((4,)), dma((CHUNKS,)), dma((CHUNKS,)), dma((CHUNKS,)), dma((5,)), dma((4,)), dma((16,)),
        ],
        compiler_params=pltpu.CompilerParams(
            collective_id=0, has_side_effects=True, vmem_limit_bytes=48 << 20
        ),
    )(snapshot)


def tree(terms):
    while len(terms) > 1:
        terms = [sum(terms[i + 1 : i + 2], terms[i]) for i in range(0, len(terms), 2)]
    return terms[0]


def unit_lower_inverse(rows, tmp):
    tile = (8, 128)
    lane = lax.broadcasted_iota(jnp.int32, tile, 1)
    sub = lax.broadcasted_iota(jnp.int32, tile, 0)
    rows, done = list(rows), []

    def lanes(v, k):
        return jnp.broadcast_to(v[:, k : k + 1], tile)

    def subs(v, k):
        return jnp.broadcast_to(v[k : k + 1, :], tile)

    for g in range(16):
        v = rows[g]
        inside = (lane >= 8 * g) & (lane < 8 * g + 8)
        cols = [lanes(v, 8 * g + k) for k in range(8)]
        base = 256 * (g % 2)
        for k in range(8):
            tmp[base + 8 * k : base + 8 * k + 8, :] = cols[k]
        def row(r):
            return tmp[pl.ds(base + r, 8, stride=0), :]
        a = [[row(8 * k + i) if i >= k else None for k in range(8)] for i in range(8)]
        n = [[None] * 8 for _ in range(8)]
        m = [[None] * 8 for _ in range(8)]
        inv = [None] * 8
        for k in range(8):
            inv[k] = 1.0 / a[k][k]
            for i in range(k + 1, 8):
                m[i][k] = a[i][k] * inv[k]
                for j in range(k + 1, i + 1):
                    a[i][j] = a[i][j] - m[i][k] * a[j][k]
        for j in range(8):
            for i in range(j + 1, 8):
                s = m[i][j]
                for t in range(j + 1, i):
                    s = s + m[i][t] * n[t][j]
                n[i][j] = -s
        vt = jnp.where(inside, jnp.where(lane == 8 * g + sub, 1.0, 0.0), v)
        tmp[base + 64 : base + 72, :] = vt
        terms = [vt]
        for k in range(7):
            col = jnp.zeros(tile, jnp.float32)
            for i in range(k + 1, 8):
                col = jnp.where(sub == i, n[i][k], col)
            terms.append(col * row(64 + k))
        p = tree(terms)
        scale = inv[0]
        for i in range(1, 8):
            scale = jnp.where(sub == i, inv[i], scale)
        q = p * scale
        tmp[base + 72 : base + 80, :] = q
        qb = [row(72 + i) for i in range(8)]
        tb = []
        for j in range(8):
            tb.append(tree([qb[j]] + [n[i][j] * qb[i] for i in range(j + 1, 8)]))
        done.append(jnp.where(lane < 8 * g + 8, p, 0.0))
        for i in range(g + 1, 16):
            vi = rows[i]
            c = [lanes(vi, 8 * g + k) for k in range(8)]
            vi = jnp.where(inside, 0.0, vi)
            rows[i] = vi - tree([c[k] * tb[k] for k in range(8)])
    return done


def eliminate(a, tmp):
    n = a.shape[1]
    inv = jnp.concatenate(unit_lower_inverse([a[8 * g : 8 * g + 8, :128] for g in range(16)], tmp), axis=0)
    s = jnp.dot(inv, a, precision=HIGHEST, preferred_element_type=jnp.float32)
    row = lax.broadcasted_iota(jnp.int32, (128, n), 0)
    lane = lax.broadcasted_iota(jnp.int32, (128, n), 1)
    s = jnp.where(lane >= row, s, 0.0)
    d = jnp.sum(jnp.where(lane[:, :128] == row[:, :128], s[:, :128], 0.0), axis=1, keepdims=True)
    return s, d


def unit_rows(s, d):
    r = s * (1.0 / jnp.sqrt(d))
    return r * (1.0 / jnp.sqrt(jnp.sum(r * r, axis=1, keepdims=True)))


def factor_rows(g_ref, ft_ref, tmp):
    s1, d1 = eliminate(g_ref[:128, :], tmp)
    ft_ref[:128, :] = unit_rows(s1, d1)
    right = s1[:, 128:]
    schur = lax.dot_general(right[:, :128] * (1.0 / d1), right, (((0,), (0,)), ((), ())),
        precision=HIGHEST, preferred_element_type=jnp.float32)
    s2, d2 = eliminate(g_ref[128:, 128:] - schur, tmp)
    ft_ref[128:, :128] = jnp.zeros((128, 128), jnp.float32)
    ft_ref[128:, 128:] = unit_rows(s2, d2)


def split(v):
    high = v.astype(jnp.bfloat16)
    return high, (v - high.astype(jnp.float32)).astype(jnp.bfloat16)


def core_kernel(
    u_ref, g_ref, core_ref, factor_ref, ubuf, cbuf, ft, fbuf, tmp, in_sem, out_sem
):
    def begin(ch, carry):
        pltpu.make_async_copy(u_ref.at[ch], ubuf.at[ch], in_sem.at[ch]).start()
        return carry

    lax.fori_loop(0, CHUNKS, begin, 0)
    factor_rows(g_ref, ft, tmp)
    high, low = split(ft[...])
    dot = functools.partial(jnp.dot, preferred_element_type=jnp.float32)
    flat = cbuf.reshape(NYD * RANK * 8, 128)

    def end(ch, carry):
        pltpu.make_async_copy(u_ref.at[ch], ubuf.at[ch], in_sem.at[ch]).wait()
        return carry

    lax.fori_loop(0, CHUNKS, end, 0)
    for y in range(NYD):
        for zz in range(0, 8, 2):
            cells = [ubuf[2 * y + (zz + k) // 4, (zz + k) % 4].reshape(ROWS, 128) for k in range(2)]
            ah, al = split(jnp.concatenate(cells, axis=1))
            out = dot(high, ah) + (dot(high, al) + dot(low, ah))
            for k in range(2):
                start = y * RANK * 8 + zz + k
                flat[pl.ds(start, RANK, stride=8), :] = out[:, 128 * k : 128 * k + 128]
        pltpu.make_async_copy(cbuf.at[y], core_ref.at[:, y], out_sem.at[y]).start()
        if y == 0:
            for k in range(4):
                fbuf[128 * k : 128 * k + 128, :] = ft[:, 128 * k : 128 * k + 128].T
            pltpu.make_async_copy(fbuf, factor_ref, out_sem.at[NYD]).start()
    for y in range(NYD):
        pltpu.make_async_copy(cbuf.at[y], core_ref.at[:, y], out_sem.at[y]).wait()
    pltpu.make_async_copy(fbuf, factor_ref, out_sem.at[NYD]).wait()


def project(u, gram):
    f32 = jnp.float32
    return pl.pallas_call(
        core_kernel,
        name="project",
        out_shape=(
            jax.ShapeDtypeStruct((RANK, NYD, 8, 128), f32),
            jax.ShapeDtypeStruct((ROWS, RANK), f32),
        ),
        in_specs=[pl.BlockSpec(memory_space=pl.ANY), pl.BlockSpec(memory_space=pltpu.VMEM)],
        out_specs=(pl.BlockSpec(memory_space=pl.ANY), pl.BlockSpec(memory_space=pl.ANY)),
        scratch_shapes=[
            pltpu.VMEM((CHUNKS, 4, WIDE, 8, 128), f32),
            pltpu.VMEM((NYD, RANK, 8, 128), f32),
            pltpu.VMEM((RANK, ROWS), f32),
            pltpu.VMEM((ROWS, RANK), f32),
            pltpu.VMEM((512, 128), f32),
            pltpu.SemaphoreType.DMA((CHUNKS,)),
            pltpu.SemaphoreType.DMA((NYD + 1,)),
        ],
        compiler_params=pltpu.CompilerParams(vmem_limit_bytes=48 << 20),
    )(u, gram)


def on_device(snapshot):
    u, gram = exchange_gram(snapshot)
    return project(u, gram)


def solution(mesh):
    in_specs = (P("wide", "narrow", None, None),)
    out_specs = (P(None, "narrow", "wide", None), P())
    return jax.shard_map(
        on_device, mesh=mesh, in_specs=in_specs, out_specs=out_specs, check_vma=False
    )
```

```python
import functools

import jax
import jax.numpy as jnp
from jax import lax
from jax.experimental import pallas as pl
from jax.experimental.pallas import tpu as pltpu
from jax.sharding import PartitionSpec as P

RANK = 256
ROWS = 512
NZD, NXD, NCD, NYD = 8, 4, 2, 4
WIDE = NZD * NXD * NCD
CHUNKS = 8
PLANE = (
    (2, 2), (2, 1), (2, 3), (1, 2), (3, 2), (1, 1), (1, 3), (3, 1),
    (3, 3), (0, 2), (2, 0), (0, 1), (0, 3), (1, 0), (3, 0),
)
MESH = pl.DeviceIdType.MESH
HIGHEST = lax.Precision.HIGHEST


def exchange_gram_kernel(
    x_ref, u_ref, g_ref,
    xin, stag, ubuf, gacc, r1, h2, r2, r3, gfull,
    in_sem, a_send, a_recv, out_sem, red_send, red_recv, piece_recv,
):
    w = lax.axis_index("wide")
    y = lax.axis_index("narrow")
    z, x, c = w // 8, (w // 2) % 4, w % 2
    piece = x * NYD + y

    def wide_id(zz, xx, cc):
        return zz * 8 + xx * 2 + cc

    barrier = pltpu.get_barrier_semaphore()

    def greet(i, carry):
        pl.semaphore_signal(barrier, inc=1, device_id=((w + i) % WIDE, y), device_id_type=MESH)
        return carry

    lax.fori_loop(24, WIDE, greet, 0)
    lax.fori_loop(1, 24, greet, 0)

    def greet_plane(i, carry):
        yy, xx = (y + 1 + i // NXD) % NYD, i % NXD
        pl.semaphore_signal(
            barrier, inc=1, device_id=(wide_id(z, xx, c), yy), device_id_type=MESH
        )
        return carry

    lax.fori_loop(0, (NYD - 1) * NXD, greet_plane, 0)

    def load(i, carry):
        yy, r = i // 8, i % 8
        pltpu.make_async_copy(
            x_ref.at[r, yy], xin.at[pl.ds(pl.multiple_of(i * 512, 512), 512)], in_sem.at[yy]
        ).start()
        return carry

    lax.fori_loop(0, 32, load, 0)

    def relayout(ch):
        yy, zh = ch // 2, ch % 2
        base = yy * 4096 + zh * 4

        def body(d, carry):
            for q in range(4):
                stag[ch, d, q] = xin[pl.ds(base + d * 8 + q, 8, stride=512), :]
            return carry

        lax.fori_loop(0, WIDE, body, 0, unroll=4)
        for q in range(4):
            ubuf[ch, q, w] = stag[ch, w, q]

    def wait_in(yy):
        whole = xin.at[pl.ds(pl.multiple_of(yy * 4096, 4096), 4096)]
        pltpu.make_async_copy(whole, whole, in_sem.at[yy]).wait()

    def send(ch):
        def body(i, carry):
            off = (i * 27) % WIDE
            t = wide_id((z + off // 8) % NZD, (x + (off // 2) % 4) % NXD, (c + off % 2) % NCD)
            pltpu.make_async_remote_copy(
                src_ref=stag.at[ch, t],
                dst_ref=ubuf.at[ch, :, w],
                send_sem=a_send.at[ch],
                recv_sem=a_recv.at[ch],
                device_id=(t, y),
                device_id_type=MESH,
            ).start()
            return carry

        lax.fori_loop(1, WIDE, body, 0)

    wait_in(0)
    relayout(0)
    pl.semaphore_wait(barrier, WIDE - 1 + (NYD - 1) * NXD)
    send(0)
    relayout(1)
    send(1)

    def send_two(yy, carry):
        wait_in(yy)
        for zh in range(2):
            relayout(yy * 2 + zh)
            send(yy * 2 + zh)
        return carry

    lax.fori_loop(1, 4, send_two, 0)

    gacc[...] = jnp.zeros_like(gacc)

    def gram(ch, carry):
        got = ubuf.at[ch, :, pl.ds(0, WIDE - 1)]
        pltpu.make_async_copy(got, got, a_recv.at[ch]).wait()
        pltpu.make_async_copy(ubuf.at[ch], u_ref.at[ch], out_sem.at[ch]).start()
        for q in range(0, 4, 2):
            left = ubuf[ch, q].reshape(ROWS, 128)
            right = ubuf[ch, q + 1].reshape(ROWS, 128)
            a = jnp.concatenate([left, right], axis=1)
            part = lax.dot_general(
                a[:RANK], a, (((1,), (1,)), ((), ())),
                precision=HIGHEST, preferred_element_type=jnp.float32,
            )
            gacc[...] += part.reshape(2, 16, 8, ROWS)
        return carry

    lax.fori_loop(0, CHUNKS, gram, 0)

    partner = wide_id(z, x, 1 - c)
    pltpu.make_async_remote_copy(
        src_ref=gacc.at[1 - c], dst_ref=r1, send_sem=red_send.at[0], recv_sem=red_recv.at[0],
        device_id=(partner, y), device_id_type=MESH,
    ).start()
    pltpu.make_async_copy(r1, r1, red_recv.at[0]).wait()
    h2[...] = gacc[c] + r1[...]

    for dx, dy in PLANE:
        xx, yy = (x + dx) % NXD, (y + dy) % NYD
        pltpu.make_async_remote_copy(
            src_ref=h2.at[xx * NYD + yy], dst_ref=r2.at[piece], send_sem=red_send.at[1],
            recv_sem=red_recv.at[1], device_id=(wide_id(z, xx, c), yy), device_id_type=MESH,
        ).start()
    r2[piece] = h2[piece]
    got = r2.at[pl.ds(0, 15)]
    pltpu.make_async_copy(got, got, red_recv.at[1]).wait()
    total = r2[0]
    for i in range(1, 16):
        total = total + r2[i]
    r3[z] = total

    def along_z(i, carry):
        zz = (z + i) % NZD
        pltpu.make_async_remote_copy(
            src_ref=r3.at[z], dst_ref=r3.at[z], send_sem=red_send.at[2],
            recv_sem=red_recv.at[2], device_id=(wide_id(zz, x, c), y), device_id_type=MESH,
        ).start()
        return carry

    lax.fori_loop(1, NZD, along_z, 0)
    got = r3.at[pl.ds(0, NZD - 1)]
    pltpu.make_async_copy(got, got, red_recv.at[2]).wait()
    total = r3[0]
    for i in range(1, NZD):
        total = total + r3[i]
    gfull[c, piece] = total

    def across(p):
        pltpu.make_async_remote_copy(
            src_ref=gfull.at[c, p], dst_ref=gfull.at[c, p], send_sem=red_send.at[4],
            recv_sem=red_recv.at[3], device_id=(partner, y), device_id_type=MESH,
        ).start()

    for dx, dy in PLANE:
        xx, yy = (x + dx) % NXD, (y + dy) % NYD
        pltpu.make_async_remote_copy(
            src_ref=gfull.at[c, piece], dst_ref=gfull.at[c, piece], send_sem=red_send.at[3],
            recv_sem=piece_recv.at[piece], device_id=(wide_id(z, xx, c), yy), device_id_type=MESH,
        ).start()
    across(piece)
    for dx, dy in PLANE[::-1]:
        p = ((x + NXD - dx) % NXD) * NYD + (y + NYD - dy) % NYD
        pltpu.make_async_copy(gfull.at[c, p], gfull.at[c, p], piece_recv.at[p]).wait()
        across(p)
    pltpu.make_async_copy(gfull.at[0], gfull.at[0], red_recv.at[3]).wait()
    g_ref[...] = gfull[...].reshape(RANK, ROWS)

    def drain(ch, carry):
        sent = stag.at[ch, pl.ds(0, WIDE - 1)]
        pltpu.make_async_copy(sent, sent, a_send.at[ch]).wait()
        pltpu.make_async_copy(ubuf.at[ch], u_ref.at[ch], out_sem.at[ch]).wait()
        return carry

    lax.fori_loop(0, CHUNKS, drain, 0)
    pltpu.make_async_copy(r1, r1, red_send.at[0]).wait()
    sent = h2.at[pl.ds(0, 15)]
    pltpu.make_async_copy(sent, sent, red_send.at[1]).wait()
    sent = r3.at[pl.ds(0, NZD - 1)]
    pltpu.make_async_copy(sent, sent, red_send.at[2]).wait()
    sent = gfull.at[c, pl.ds(0, 15)]
    pltpu.make_async_copy(sent, sent, red_send.at[3]).wait()
    pltpu.make_async_copy(gfull.at[0], gfull.at[0], red_send.at[4]).wait()


def exchange_gram(snapshot):
    f32 = jnp.float32
    dma = pltpu.SemaphoreType.DMA
    return pl.pallas_call(
        exchange_gram_kernel,
        name="exchange_gram",
        out_shape=(
            jax.ShapeDtypeStruct((CHUNKS, 4, WIDE, 8, 128), f32),
            jax.ShapeDtypeStruct((RANK, ROWS), f32),
        ),
        in_specs=[pl.BlockSpec(memory_space=pl.ANY)],
        out_specs=(
            pl.BlockSpec(memory_space=pl.ANY),
            pl.BlockSpec(memory_space=pltpu.VMEM),
        ),
        scratch_shapes=[
            pltpu.VMEM((4 * 8 * 512, 128), f32),
            pltpu.VMEM((CHUNKS, WIDE, 4, 8, 128), f32),
            pltpu.VMEM((CHUNKS, 4, WIDE, 8, 128), f32),
            pltpu.VMEM((2, 16, 8, ROWS), f32),
            pltpu.VMEM((16, 8, ROWS), f32),
            pltpu.VMEM((16, 8, ROWS), f32),
            pltpu.VMEM((16, 8, ROWS), f32),
            pltpu.VMEM((NZD, 8, ROWS), f32),
            pltpu.VMEM((2, 16, 8, ROWS), f32),
            dma((4,)), dma((CHUNKS,)), dma((CHUNKS,)), dma((CHUNKS,)), dma((5,)), dma((4,)), dma((16,)),
        ],
        compiler_params=pltpu.CompilerParams(
            collective_id=0, has_side_effects=True, vmem_limit_bytes=48 << 20
        ),
    )(snapshot)


def tree(terms):
    while len(terms) > 1:
        terms = [sum(terms[i + 1 : i + 2], terms[i]) for i in range(0, len(terms), 2)]
    return terms[0]


def unit_lower_inverse(rows, tmp):
    tile = (8, 128)
    lane = lax.broadcasted_iota(jnp.int32, tile, 1)
    sub = lax.broadcasted_iota(jnp.int32, tile, 0)
    rows, done = list(rows), []

    def lanes(v, k):
        return jnp.broadcast_to(v[:, k : k + 1], tile)

    def subs(v, k):
        return jnp.broadcast_to(v[k : k + 1, :], tile)

    for g in range(16):
        v = rows[g]
        inside = (lane >= 8 * g) & (lane < 8 * g + 8)
        cols = [lanes(v, 8 * g + k) for k in range(8)]
        base = 256 * (g % 2)
        for k in range(8):
            tmp[base + 8 * k : base + 8 * k + 8, :] = cols[k]
        def row(r):
            return tmp[pl.ds(base + r, 8, stride=0), :]
        a = [[row(8 * k + i) if i >= k else None for k in range(8)] for i in range(8)]
        n = [[None] * 8 for _ in range(8)]
        m = [[None] * 8 for _ in range(8)]
        inv = [None] * 8
        for k in range(8):
            inv[k] = 1.0 / a[k][k]
            for i in range(k + 1, 8):
                m[i][k] = a[i][k] * inv[k]
                for j in range(k + 1, i + 1):
                    a[i][j] = a[i][j] - m[i][k] * a[j][k]
        for j in range(8):
            for i in range(j + 1, 8):
                s = m[i][j]
                for t in range(j + 1, i):
                    s = s + m[i][t] * n[t][j]
                n[i][j] = -s
        vt = jnp.where(inside, jnp.where(lane == 8 * g + sub, 1.0, 0.0), v)
        tmp[base + 64 : base + 72, :] = vt
        terms = [vt]
        for k in range(7):
            col = jnp.zeros(tile, jnp.float32)
            for i in range(k + 1, 8):
                col = jnp.where(sub == i, n[i][k], col)
            terms.append(col * row(64 + k))
        p = tree(terms)
        scale = inv[0]
        for i in range(1, 8):
            scale = jnp.where(sub == i, inv[i], scale)
        q = p * scale
        tmp[base + 72 : base + 80, :] = q
        qb = [row(72 + i) for i in range(8)]
        tb = []
        for j in range(8):
            tb.append(tree([qb[j]] + [n[i][j] * qb[i] for i in range(j + 1, 8)]))
        done.append(jnp.where(lane < 8 * g + 8, p, 0.0))
        for i in range(g + 1, 16):
            vi = rows[i]
            c = [lanes(vi, 8 * g + k) for k in range(8)]
            vi = jnp.where(inside, 0.0, vi)
            rows[i] = vi - tree([c[k] * tb[k] for k in range(8)])
    return done


def eliminate(a, tmp):
    n = a.shape[1]
    inv = jnp.concatenate(unit_lower_inverse([a[8 * g : 8 * g + 8, :128] for g in range(16)], tmp), axis=0)
    s = jnp.dot(inv, a, precision=HIGHEST, preferred_element_type=jnp.float32)
    row = lax.broadcasted_iota(jnp.int32, (128, n), 0)
    lane = lax.broadcasted_iota(jnp.int32, (128, n), 1)
    s = jnp.where(lane >= row, s, 0.0)
    d = jnp.sum(jnp.where(lane[:, :128] == row[:, :128], s[:, :128], 0.0), axis=1, keepdims=True)
    return s, d


def unit_rows(s, d):
    r = s * (1.0 / jnp.sqrt(d))
    return r * (1.0 / jnp.sqrt(jnp.sum(r * r, axis=1, keepdims=True)))


def factor_rows(g_ref, ft_ref, tmp):
    s1, d1 = eliminate(g_ref[:128, :], tmp)
    ft_ref[:128, :] = unit_rows(s1, d1)
    right = s1[:, 128:]
    schur = lax.dot_general(right[:, :128] * (1.0 / d1), right, (((0,), (0,)), ((), ())),
        precision=HIGHEST, preferred_element_type=jnp.float32)
    s2, d2 = eliminate(g_ref[128:, 128:] - schur, tmp)
    ft_ref[128:, :128] = jnp.zeros((128, 128), jnp.float32)
    ft_ref[128:, 128:] = unit_rows(s2, d2)


def split(v):
    high = v.astype(jnp.bfloat16)
    return high, (v - high.astype(jnp.float32)).astype(jnp.bfloat16)


def core_kernel(
    u_ref, g_ref, core_ref, factor_ref, ubuf, cbuf, ft, fbuf, tmp, in_sem, out_sem
):
    def begin(ch, carry):
        pltpu.make_async_copy(u_ref.at[ch], ubuf.at[ch], in_sem.at[ch]).start()
        return carry

    lax.fori_loop(0, CHUNKS, begin, 0)
    factor_rows(g_ref, ft, tmp)
    high, low = split(ft[...])
    dot = functools.partial(jnp.dot, preferred_element_type=jnp.float32)
    flat = cbuf.reshape(NYD * RANK * 8, 128)

    def end(ch, carry):
        pltpu.make_async_copy(u_ref.at[ch], ubuf.at[ch], in_sem.at[ch]).wait()
        return carry

    lax.fori_loop(0, CHUNKS, end, 0)
    for y in range(NYD):
        for zz in range(0, 8, 2):
            cells = [ubuf[2 * y + (zz + k) // 4, (zz + k) % 4].reshape(ROWS, 128) for k in range(2)]
            ah, al = split(jnp.concatenate(cells, axis=1))
            out = dot(high, ah) + (dot(high, al) + dot(low, ah))
            for k in range(2):
                start = y * RANK * 8 + zz + k
                flat[pl.ds(start, RANK, stride=8), :] = out[:, 128 * k : 128 * k + 128]
        pltpu.make_async_copy(cbuf.at[y], core_ref.at[:, y], out_sem.at[y]).start()
        if y == 0:
            for k in range(4):
                fbuf[128 * k : 128 * k + 128, :] = ft[:, 128 * k : 128 * k + 128].T
            pltpu.make_async_copy(fbuf, factor_ref, out_sem.at[NYD]).start()
    for y in range(NYD):
        pltpu.make_async_copy(cbuf.at[y], core_ref.at[:, y], out_sem.at[y]).wait()
    pltpu.make_async_copy(fbuf, factor_ref, out_sem.at[NYD]).wait()


def project(u, gram):
    f32 = jnp.float32
    return pl.pallas_call(
        core_kernel,
        name="project",
        out_shape=(
            jax.ShapeDtypeStruct((RANK, NYD, 8, 128), f32),
            jax.ShapeDtypeStruct((ROWS, RANK), f32),
        ),
        in_specs=[pl.BlockSpec(memory_space=pl.ANY), pl.BlockSpec(memory_space=pltpu.VMEM)],
        out_specs=(pl.BlockSpec(memory_space=pl.ANY), pl.BlockSpec(memory_space=pl.ANY)),
        scratch_shapes=[
            pltpu.VMEM((CHUNKS, 4, WIDE, 8, 128), f32),
            pltpu.VMEM((NYD, RANK, 8, 128), f32),
            pltpu.VMEM((RANK, ROWS), f32),
            pltpu.VMEM((ROWS, RANK), f32),
            pltpu.VMEM((512, 128), f32),
            pltpu.SemaphoreType.DMA((CHUNKS,)),
            pltpu.SemaphoreType.DMA((NYD + 1,)),
        ],
        compiler_params=pltpu.CompilerParams(vmem_limit_bytes=48 << 20),
    )(u, gram)


def on_device(snapshot):
    u, gram = exchange_gram(snapshot)
    return project(u, gram)


def solution(mesh):
    in_specs = (P("wide", "narrow", None, None),)
    out_specs = (P(None, "narrow", "wide", None), P())
    return jax.shard_map(
        on_device, mesh=mesh, in_specs=in_specs, out_specs=out_specs, check_vma=False
    )
```
